128 devices in a mesh: dp: 8 (over z_lo, y), tensor: 16 (over x, z_hi, core).
Axes of the slice: x: 4, y: 4, z: 4 (z_hi: 2, z_lo: 2; z = z_hi * 2 + z_lo), core: 2. Of those that a mesh axis runs over, the one named last changes fastest.
Arguments:
- hidden: bfloat16 [1024, 8192], P('dp', 'tensor')
- norm_gain: float32 [8192], P('tensor'), may hold values from 0.5 to 1.5
- head: bfloat16 [8192, 147456], P(None, ('dp', 'tensor'))
- targets: int32 [1024], P('dp'), may hold values from 0 to 147455
- old_logprob: float32 [1024], P('dp'), may hold values from -20 to -1
- lengths: int32 [8], P('dp'), may hold values from 1 to 128, as said below
Outputs:
- new_logprob: float32 [1024], P('dp')
- log_ratio: float32 [1024], P('dp')
The draws below stay inside these ranges and needn't reach their ends.
Inputs may be any that keep to these rules, and one draw needn't show every extreme that they name: `lengths`: every length is at least 1 and at most 128; some sequence has 128 live tokens and some has 1.
All inputs are finite; a program needn't handle non-finite values.
Results may differ from the reference program's by a relative error of at most 0.00094.
Values may be sent and summed in bfloat16 or wider, within the bound.
A program may use at most 128 MiB of HBM per device.

```python
import jax
import jax.numpy as jnp
from jax import lax

D = 8192
V_DEV = 1152
LEN = 128
TOKENS = 1024
SEQS = 8
VOCAB = 147456
DEVICES = 128


def draw_hidden(key, part):
    first, second = jax.random.split(key, 2)
    ramp = jnp.exp(jnp.log(3.0) * jnp.arange(D, dtype=jnp.float32) / D)
    base = jax.random.normal(first, (TOKENS, D), jnp.float32)
    scales = jnp.exp(jax.random.uniform(second, (TOKENS, 1), jnp.float32, 0.0, jnp.log(10.0)))
    return (base * scales * ramp[None, :]).astype(jnp.bfloat16)


def draw_head(key, part):
    first, second = jax.random.split(key, 2)
    base = jax.random.normal(first, (D, VOCAB), jnp.float32)
    columns = jnp.exp(jax.random.uniform(second, (1, VOCAB), jnp.float32, 0.0, jnp.log(4.0)))
    return (base * columns * (3.0 / jnp.sqrt(jnp.float32(D)))).astype(jnp.bfloat16)


def draw_lengths(key, part):
    first, second = jax.random.split(key, 2)
    values = jax.random.randint(first, (SEQS,), 1, LEN + 1, jnp.int32)
    order = jax.random.permutation(second, SEQS)
    values = values.at[order[0]].set(LEN)
    values = values.at[order[1]].set(1)
    return values


def plant(entries, key, smallest, top_value):
    dims = entries.shape
    spot = [jax.random.randint(jax.random.fold_in(key, axis), (), 0, dims[axis]) for axis in range(len(dims))]
    entries = entries.at[tuple(spot)].set(smallest)
    longest = dims.index(max(dims))
    spot[longest] = (spot[longest] + 1) % dims[longest]
    return entries.at[tuple(spot)].set(top_value)


def shard_levels(own_key, shape, shards, low, top_value):
    def one(dim, parts):
        steps = jax.random.uniform(jax.random.fold_in(jax.random.fold_in(own_key, 6), dim), (parts,), jnp.float32, low / len(shards), top_value / len(shards))
        return jnp.repeat(jnp.exp(steps), shape[dim] // parts).reshape((-1,) + (1,) * (len(shape) - dim - 1))

    factor_of = one(*shards[0])
    for cut in shards[1:]:
        factor_of = factor_of * one(*cut)
    return factor_of


def setup_inputs(seed: int = 0) -> dict:
    key_of = jax.random.split(jax.random.key(seed), 7)
    hidden = draw_hidden(jax.random.fold_in(key_of[6], 71), 0)
    norm_gain = jnp.clip(1.0 + 0.1 * jax.random.normal(key_of[1], (D,), jnp.float32), 0.5, 1.5)
    head = draw_head(jax.random.fold_in(key_of[6], 71), 0)
    targets = plant(jax.random.randint(key_of[3], (TOKENS,), 0, VOCAB), jax.random.fold_in(key_of[3], 1), 0, VOCAB - 1).astype(jnp.int32)
    old_logprob = jnp.clip(-20.0 + 19.0 * jax.random.uniform(key_of[4], (TOKENS,), jnp.float32) ** shard_levels(key_of[4], (TOKENS,), ((0, 8),), -0.2, 0.2), -20.0, -1.0)
    lengths = draw_lengths(jax.random.fold_in(key_of[6], 71), 0)
    return {"hidden": hidden, "norm_gain": norm_gain, "head": head, "targets": targets, "old_logprob": old_logprob, "lengths": lengths}


def reference(hidden, norm_gain, head, targets, old_logprob, lengths):
    values = hidden.astype(jnp.float32)
    mean_sq = lax.optimization_barrier(jnp.mean(values * values, axis=1, keepdims=True))
    normed = (values * lax.rsqrt(mean_sq + 1e-06) * norm_gain[None, :]).astype(jnp.bfloat16)
    count = normed.shape[0]

    def block_step(carry, block):
        top, total, picked = carry
        start = (block * V_DEV).astype(jnp.int32)
        weights = lax.dynamic_slice_in_dim(head, start, V_DEV, 1)
        logits = jnp.dot(normed, weights, preferred_element_type=jnp.float32)
        block_top = lax.optimization_barrier(jnp.max(logits, axis=1))
        new_top = jnp.maximum(top, block_top)
        total = total * jnp.exp(top - new_top) + lax.optimization_barrier(jnp.sum(jnp.exp(logits - new_top[:, None]), axis=1))
        column = start + jnp.arange(V_DEV, dtype=jnp.int32)
        hits = column[None, :] == targets[:, None]
        picked = picked + lax.optimization_barrier(jnp.sum(jnp.where(hits, logits, jnp.float32(0.0)), axis=1))
        return ((new_top, total, picked), None)
    init = (jnp.full((count,), -jnp.inf, jnp.float32), jnp.zeros((count,), jnp.float32), jnp.zeros((count,), jnp.float32))
    (top, total, picked), _ = lax.scan(block_step, init, jnp.arange(DEVICES, dtype=jnp.int32))
    position = jnp.arange(LEN, dtype=jnp.int32)
    live = (position[None, :] < lengths[:, None]).reshape(-1).astype(jnp.float32)
    logprob = picked - top - jnp.log(total)
    return (live * logprob, live * (logprob - old_logprob))
```

```python
import functools

import jax
import jax.numpy as jnp
from jax import lax
from jax.experimental import pallas as pl
from jax.experimental.pallas import tpu as pltpu
from jax.sharding import PartitionSpec as P

MESH = pl.DeviceIdType.MESH


def _barrier(nd, nt, d, t):
    barrier = pltpu.get_barrier_semaphore()
    for k in range(1, nd):
        pl.semaphore_signal(barrier, inc=1, device_id=(lax.rem(d + k, nd), t), device_id_type=MESH)
    for k in range(1, nt):
        pl.semaphore_signal(barrier, inc=1, device_id=(d, lax.rem(t + k, nt)), device_id_type=MESH)
    pl.semaphore_wait(barrier, nd - 1 + nt - 1)


def _pre_kernel(nd, nt, ssq_ref, tgt_ref, q_out, t_out, q_buf, t_buf, q_send, q_recv, t_send, t_recv, local):
    d = lax.axis_index("dp")
    t = lax.axis_index("tensor")
    _barrier(nd, nt, d, t)
    own_q = pltpu.make_async_copy(ssq_ref, q_buf.at[t], local.at[0])
    own_t = pltpu.make_async_copy(tgt_ref, t_buf.at[d], local.at[1])
    own_q.start()
    own_t.start()
    sends = []
    for k in range(1, nt):
        c = pltpu.make_async_remote_copy(
            src_ref=ssq_ref, dst_ref=q_buf.at[t], send_sem=q_send.at[k], recv_sem=q_recv.at[t],
            device_id=(d, lax.rem(t + k, nt)), device_id_type=MESH)
        c.start()
        sends.append(c)
    for k in range(1, nd):
        c = pltpu.make_async_remote_copy(
            src_ref=tgt_ref, dst_ref=t_buf.at[d], send_sem=t_send.at[k], recv_sem=t_recv.at[d],
            device_id=(lax.rem(d + k, nd), t), device_id_type=MESH)
        c.start()
        sends.append(c)
    for k in range(1, nt):
        src = lax.rem(t + nt - k, nt)
        pltpu.make_async_remote_copy(
            src_ref=ssq_ref, dst_ref=q_buf.at[src], send_sem=q_send.at[k], recv_sem=q_recv.at[src],
            device_id=(d, src), device_id_type=MESH).wait_recv()
    for k in range(1, nd):
        src = lax.rem(d + nd - k, nd)
        pltpu.make_async_remote_copy(
            src_ref=tgt_ref, dst_ref=t_buf.at[src], send_sem=t_send.at[k], recv_sem=t_recv.at[src],
            device_id=(src, t), device_id_type=MESH).wait_recv()
    for c in sends:
        c.wait_send()
    own_q.wait()
    own_t.wait()
    q_out[...] = q_buf[...]
    t_out[...] = t_buf[...]


def _stats_kernel(nd, nt, s_ref, out_ref, r1, r2, s1_send, s1_recv, s2_send, s2_recv, local):
    d = lax.axis_index("dp")
    t = lax.axis_index("tensor")
    _barrier(nd, nt, d, t)
    own1 = pltpu.make_async_copy(s_ref.at[d], r1.at[d], local.at[0])
    own1.start()
    sends = []
    for k in range(1, nd):
        peer = lax.rem(d + k, nd)
        c = pltpu.make_async_remote_copy(
            src_ref=s_ref.at[peer], dst_ref=r1.at[d], send_sem=s1_send.at[k], recv_sem=s1_recv.at[d],
            device_id=(peer, t), device_id_type=MESH)
        c.start()
        sends.append(c)
    for k in range(1, nd):
        src = lax.rem(d + nd - k, nd)
        pltpu.make_async_remote_copy(
            src_ref=s_ref.at[0], dst_ref=r1.at[src], send_sem=s1_send.at[k], recv_sem=s1_recv.at[src],
            device_id=(src, t), device_id_type=MESH).wait_recv()
    own1.wait()
    own2 = pltpu.make_async_copy(r1, r2.at[t], local.at[1])
    own2.start()
    for k in range(1, nt):
        c = pltpu.make_async_remote_copy(
            src_ref=r1, dst_ref=r2.at[t], send_sem=s2_send.at[k], recv_sem=s2_recv.at[t],
            device_id=(d, lax.rem(t + k, nt)), device_id_type=MESH)
        c.start()
        sends.append(c)
    for k in range(1, nt):
        src = lax.rem(t + nt - k, nt)
        pltpu.make_async_remote_copy(
            src_ref=r1, dst_ref=r2.at[src], send_sem=s2_send.at[k], recv_sem=s2_recv.at[src],
            device_id=(d, src), device_id_type=MESH).wait_recv()
    for c in sends:
        c.wait_send()
    own2.wait()
    out_ref[...] = r2[...]


def _vmem_call(kernel, out_shape, scratch, cid):
    n_out = len(out_shape) if isinstance(out_shape, (tuple, list)) else 1
    out_specs = [pl.BlockSpec(memory_space=pltpu.VMEM)] * n_out
    return pl.pallas_call(
        kernel,
        out_shape=out_shape,
        out_specs=out_specs if n_out > 1 else out_specs[0],
        scratch_shapes=scratch,
        compiler_params=pltpu.CompilerParams(collective_id=cid, has_side_effects=True),
    )


def _body(nd, nt, hidden, norm_gain, head, targets, old_logprob, lengths):
    tok_rows = hidden.shape[0]
    width = hidden.shape[1] * nt
    lanes = 128
    values = hidden.astype(jnp.float32)
    part_sq = jnp.sum(values * values, axis=1)

    ssq_in = jnp.zeros((8, tok_rows), jnp.float32).at[0].set(part_sq)
    tgt_in = jnp.zeros((8, tok_rows), jnp.int32).at[0].set(targets)
    pre = _vmem_call(
        functools.partial(_pre_kernel, nd, nt),
        (jax.ShapeDtypeStruct((nt, 8, tok_rows), jnp.float32),
         jax.ShapeDtypeStruct((nd, 8, tok_rows), jnp.int32)),
        [pltpu.VMEM((nt, 8, tok_rows), jnp.float32),
         pltpu.VMEM((nd, 8, tok_rows), jnp.int32),
         pltpu.SemaphoreType.DMA((nt,)), pltpu.SemaphoreType.DMA((nt,)),
         pltpu.SemaphoreType.DMA((nd,)), pltpu.SemaphoreType.DMA((nd,)),
         pltpu.SemaphoreType.DMA((2,))],
        0,
    )
    q_all, t_all = pre(ssq_in, tgt_in)
    sum_sq = jnp.sum(q_all[:, 0, :], axis=0)
    target_all = t_all[:, 0, :].reshape(nd * tok_rows)

    scaled = lax.rsqrt(sum_sq / width + 1e-06)
    normed = (values * scaled[:, None] * norm_gain[None, :]).astype(jnp.bfloat16)
    vocab_cols = head.shape[1]
    rows = lax.all_gather(normed, "dp", axis=0, tiled=True)
    logits = jnp.dot(
        lax.all_gather(rows, "tensor", axis=1, tiled=True), head, preferred_element_type=jnp.float32
    )
    vocab_start = lax.axis_index(("dp", "tensor")) * vocab_cols
    block_top = jnp.max(logits, axis=1)
    block_total = jnp.sum(jnp.exp(logits - block_top[:, None]), axis=1)
    column = vocab_start + jnp.arange(vocab_cols, dtype=jnp.int32)
    hits = column[None, :] == target_all[:, None]
    block_pick = jnp.sum(jnp.where(hits, logits, jnp.float32(0.0)), axis=1)

    stacked = jnp.stack([block_top, block_total, block_pick], axis=0).reshape(3, nd, tok_rows)
    stacked = jnp.transpose(stacked, (1, 0, 2))
    s_in = jnp.concatenate([stacked, jnp.zeros((nd, 5, tok_rows), jnp.float32)], axis=1)
    stats = _vmem_call(
        functools.partial(_stats_kernel, nd, nt),
        jax.ShapeDtypeStruct((nt, nd, 8, tok_rows), jnp.float32),
        [pltpu.VMEM((nd, 8, tok_rows), jnp.float32),
         pltpu.VMEM((nt, nd, 8, tok_rows), jnp.float32),
         pltpu.SemaphoreType.DMA((nd,)), pltpu.SemaphoreType.DMA((nd,)),
         pltpu.SemaphoreType.DMA((nt,)), pltpu.SemaphoreType.DMA((nt,)),
         pltpu.SemaphoreType.DMA((2,))],
        1,
    )(s_in)
    pieces = stats.reshape(nt * nd, 8, tok_rows)
    tops = pieces[:, 0, :]
    top = jnp.max(tops, axis=0)
    total = jnp.sum(pieces[:, 1, :] * jnp.exp(tops - top[None, :]), axis=0)
    picked = jnp.sum(pieces[:, 2, :], axis=0)

    seq_count = lengths.shape[0]
    position = jnp.arange(tok_rows // seq_count, dtype=jnp.int32)
    live = (position[None, :] < lengths[:, None]).reshape(-1).astype(jnp.float32)
    logprob = picked - top - jnp.log(total)
    return (live * logprob, live * (logprob - old_logprob))


def solution(mesh):
    nd = mesh.shape["dp"]
    nt = mesh.shape["tensor"]
    in_specs = (
        P("dp", "tensor"),
        P("tensor"),
        P(None, ("dp", "tensor")),
        P("dp"),
        P("dp"),
        P("dp"),
    )
    out_specs = (P("dp"), P("dp"))
    return jax.shard_map(
        functools.partial(_body, nd, nt), mesh=mesh, in_specs=in_specs, out_specs=out_specs, check_vma=False
    )
```

```python
import functools

import jax
import jax.numpy as jnp
from jax import lax
from jax.experimental import pallas as pl
from jax.experimental.pallas import tpu as pltpu
from jax.sharding import PartitionSpec as P

MESH = pl.DeviceIdType.MESH


def _barrier(nd, nt, d, t):
    barrier = pltpu.get_barrier_semaphore()
    for k in range(1, nd):
        pl.semaphore_signal(barrier, inc=1, device_id=(lax.rem(d + k, nd), t), device_id_type=MESH)
    for k in range(1, nt):
        pl.semaphore_signal(barrier, inc=1, device_id=(d, lax.rem(t + k, nt)), device_id_type=MESH)
    pl.semaphore_wait(barrier, nd - 1 + nt - 1)


def _pre_kernel(nd, nt, ssq_ref, tgt_ref, q_out, t_out, q_buf, t_buf, q_send, q_recv, t_send, t_recv, local):
    d = lax.axis_index("dp")
    t = lax.axis_index("tensor")
    _barrier(nd, nt, d, t)
    own_q = pltpu.make_async_copy(ssq_ref, q_buf.at[t], local.at[0])
    own_t = pltpu.make_async_copy(tgt_ref, t_buf.at[d], local.at[1])
    own_q.start()
    own_t.start()
    sends = []
    for k in range(1, nt):
        c = pltpu.make_async_remote_copy(
            src_ref=ssq_ref, dst_ref=q_buf.at[t], send_sem=q_send.at[k], recv_sem=q_recv.at[t],
            device_id=(d, lax.rem(t + k, nt)), device_id_type=MESH)
        c.start()
        sends.append(c)
    for k in range(1, nd):
        c = pltpu.make_async_remote_copy(
            src_ref=tgt_ref, dst_ref=t_buf.at[d], send_sem=t_send.at[k], recv_sem=t_recv.at[d],
            device_id=(lax.rem(d + k, nd), t), device_id_type=MESH)
        c.start()
        sends.append(c)
    for k in range(1, nt):
        src = lax.rem(t + nt - k, nt)
        pltpu.make_async_remote_copy(
            src_ref=ssq_ref, dst_ref=q_buf.at[src], send_sem=q_send.at[k], recv_sem=q_recv.at[src],
            device_id=(d, src), device_id_type=MESH).wait_recv()
    for k in range(1, nd):
        src = lax.rem(d + nd - k, nd)
        pltpu.make_async_remote_copy(
            src_ref=tgt_ref, dst_ref=t_buf.at[src], send_sem=t_send.at[k], recv_sem=t_recv.at[src],
            device_id=(src, t), device_id_type=MESH).wait_recv()
    for c in sends:
        c.wait_send()
    own_q.wait()
    own_t.wait()
    q_out[...] = q_buf[...]
    t_out[...] = t_buf[...]


def _stats_kernel(nd, nt, s_ref, out_ref, r1, r2, s1_send, s1_recv, s2_send, s2_recv, local):
    d = lax.axis_index("dp")
    t = lax.axis_index("tensor")
    _barrier(nd, nt, d, t)
    own1 = pltpu.make_async_copy(s_ref.at[d], r1.at[d], local.at[0])
    own1.start()
    sends = []
    for k in range(1, nd):
        peer = lax.rem(d + k, nd)
        c = pltpu.make_async_remote_copy(
            src_ref=s_ref.at[peer], dst_ref=r1.at[d], send_sem=s1_send.at[k], recv_sem=s1_recv.at[d],
            device_id=(peer, t), device_id_type=MESH)
        c.start()
        sends.append(c)
    for k in range(1, nd):
        src = lax.rem(d + nd - k, nd)
        pltpu.make_async_remote_copy(
            src_ref=s_ref.at[0], dst_ref=r1.at[src], send_sem=s1_send.at[k], recv_sem=s1_recv.at[src],
            device_id=(src, t), device_id_type=MESH).wait_recv()
    own1.wait()
    own2 = pltpu.make_async_copy(r1, r2.at[t], local.at[1])
    own2.start()
    for k in range(1, nt):
        c = pltpu.make_async_remote_copy(
            src_ref=r1, dst_ref=r2.at[t], send_sem=s2_send.at[k], recv_sem=s2_recv.at[t],
            device_id=(d, lax.rem(t + k, nt)), device_id_type=MESH)
        c.start()
        sends.append(c)
    for k in range(1, nt):
        src = lax.rem(t + nt - k, nt)
        pltpu.make_async_remote_copy(
            src_ref=r1, dst_ref=r2.at[src], send_sem=s2_send.at[k], recv_sem=s2_recv.at[src],
            device_id=(d, src), device_id_type=MESH).wait_recv()
    for c in sends:
        c.wait_send()
    own2.wait()
    out_ref[...] = r2[...]


ORDERS = (("x", "y", "z"), ("y", "z", "x"), ("z", "x", "y"))
PARTS = (48, 48, 32)
RING = 4


def _wrap(v):
    return lax.rem(v + RING, RING)


def _slab(order, k, cd):
    full = (cd[order[2]], cd[order[1]], cd[order[0]])
    return full[: 3 - k]


def _gather_kernel(x_ref, o0, o1, o2, ssem, rsem, psend, precv, lsem):
    outs = (o0, o1, o2)
    d = lax.axis_index("dp")
    t = lax.axis_index("tensor")
    cc = lax.rem(t, 2)
    me = {"x": t // 4, "y": lax.rem(d, 4), "z": (lax.rem(t // 2, 2)) * 2 + d // 4}

    def dev(cd):
        return (lax.rem(cd["z"], 2) * 4 + cd["y"], cd["x"] * 4 + (cd["z"] // 2) * 2 + cc)

    def moved(dim, delta):
        cd = dict(me)
        cd[dim] = _wrap(me[dim] + delta)
        return cd

    partner = (d, t + 1 - 2 * cc)
    barrier = pltpu.get_barrier_semaphore()
    for dim in ("x", "y", "z"):
        for delta in (1, -1):
            pl.semaphore_signal(barrier, inc=1, device_id=dev(moved(dim, delta)), device_id_type=MESH)
    pl.semaphore_signal(barrier, inc=1, device_id=partner, device_id_type=MESH)
    pl.semaphore_wait(barrier, 7)

    def view(r, slot, idx, k, half):
        tail = ()
        if half is not None:
            tail = (slice(None),) * (k + 1) + (pl.ds(half * 256, 256),)
        return outs[r].at[(slot,) + idx + tail]

    fwd = []

    def to_partner(r, j, idx, k, half):
        c = pltpu.make_async_remote_copy(
            src_ref=view(r, cc, idx, k, half), dst_ref=view(r, cc, idx, k, half),
            send_sem=psend.at[r * 13 + j], recv_sem=precv.at[r * 13 + j],
            device_id=partner, device_id_type=MESH)
        c.start()
        fwd.append((c, view(r, 1 - cc, idx, k, half), r * 13 + j))

    own = []
    off = 0
    for r in range(3):
        idx = _slab(ORDERS[r], 0, me)
        c = pltpu.make_async_copy(x_ref.at[pl.ds(off, PARTS[r])], view(r, cc, idx, 0, None), lsem.at[r])
        c.start()
        own.append(c)
        off += PARTS[r]
    for r in range(3):
        own[r].wait()
        to_partner(r, 0, _slab(ORDERS[r], 0, me), 0, None)

    sends = []
    for k in range(3):
        for r in range(3):
            dim = ORDERS[r][k]
            idx = _slab(ORDERS[r], k, me)
            for di, delta in enumerate((1, -1)):
                s = (r * 3 + k) * 4 + di
                c = pltpu.make_async_remote_copy(
                    src_ref=view(r, cc, idx, k, None), dst_ref=view(r, cc, idx, k, None),
                    send_sem=ssem.at[s], recv_sem=rsem.at[s],
                    device_id=dev(moved(dim, delta)), device_id_type=MESH)
                c.start()
                sends.append(c)
        for r in range(3):
            dim = ORDERS[r][k]
            for di, delta in enumerate((1, -1)):
                s = (r * 3 + k) * 4 + di
                src_idx = _slab(ORDERS[r], k, moved(dim, -delta))
                pltpu.make_async_remote_copy(
                    src_ref=view(r, cc, src_idx, k, None), dst_ref=view(r, cc, src_idx, k, None),
                    send_sem=ssem.at[s], recv_sem=rsem.at[s],
                    device_id=dev(moved(dim, -delta)), device_id_type=MESH).wait_recv()
                to_partner(r, 1 + 4 * k + di, src_idx, k, None)
            for di, delta in enumerate((1, -1)):
                s = (r * 3 + k) * 4 + 2 + di
                src_idx = _slab(ORDERS[r], k, moved(dim, -delta))
                c = pltpu.make_async_remote_copy(
                    src_ref=view(r, cc, src_idx, k, di), dst_ref=view(r, cc, src_idx, k, di),
                    send_sem=ssem.at[s], recv_sem=rsem.at[s],
                    device_id=dev(moved(dim, delta)), device_id_type=MESH)
                c.start()
                sends.append(c)
        for r in range(3):
            dim = ORDERS[r][k]
            for di, delta in enumerate((1, -1)):
                s = (r * 3 + k) * 4 + 2 + di
                far_idx = _slab(ORDERS[r], k, moved(dim, 2))
                pltpu.make_async_remote_copy(
                    src_ref=view(r, cc, far_idx, k, di), dst_ref=view(r, cc, far_idx, k, di),
                    send_sem=ssem.at[s], recv_sem=rsem.at[s],
                    device_id=dev(moved(dim, -delta)), device_id_type=MESH).wait_recv()
                to_partner(r, 3 + 4 * k + di, far_idx, k, di)
    for c in sends:
        c.wait_send()
    for c, dst, j in fwd:
        c.wait_send()
        pltpu.make_async_remote_copy(
            src_ref=dst, dst_ref=dst, send_sem=psend.at[j], recv_sem=precv.at[j],
            device_id=partner, device_id_type=MESH).wait_recv()


def _gather(normed):
    rows, cols = normed.shape
    call = pl.pallas_call(
        _gather_kernel,
        out_shape=[jax.ShapeDtypeStruct((2, RING, RING, RING, p, cols), normed.dtype) for p in PARTS],
        in_specs=[pl.BlockSpec(memory_space=pltpu.VMEM)],
        out_specs=[pl.BlockSpec(memory_space=pl.ANY)] * 3,
        scratch_shapes=[
            pltpu.SemaphoreType.DMA((36,)), pltpu.SemaphoreType.DMA((36,)),
            pltpu.SemaphoreType.DMA((39,)), pltpu.SemaphoreType.DMA((39,)),
            pltpu.SemaphoreType.DMA((3,)),
        ],
        compiler_params=pltpu.CompilerParams(collective_id=2, has_side_effects=True),
    )
    bufs = call(normed)
    parts = []
    for r, buf in enumerate(bufs):
        a0, a1, a2 = ORDERS[r]
        names = ["c", a2, a1, a0, "i", "f"]
        zpos = names.index("z")
        shape = list(buf.shape)
        buf = buf.reshape(shape[:zpos] + [2, 2] + shape[zpos + 1:])
        names = names[:zpos] + ["h", "l"] + names[zpos + 1:]
        perm = [names.index(n) for n in ("l", "y", "i", "x", "h", "c", "f")]
        buf = jnp.transpose(buf, perm)
        parts.append(buf.reshape(2 * RING, PARTS[r], RING * 2 * 2 * cols))
    return jnp.concatenate(parts, axis=1).reshape(2 * RING * rows, RING * 2 * 2 * cols)


def _vmem_call(kernel, out_shape, scratch, cid):
    n_out = len(out_shape) if isinstance(out_shape, (tuple, list)) else 1
    out_specs = [pl.BlockSpec(memory_space=pltpu.VMEM)] * n_out
    return pl.pallas_call(
        kernel,
        out_shape=out_shape,
        out_specs=out_specs if n_out > 1 else out_specs[0],
        scratch_shapes=scratch,
        compiler_params=pltpu.CompilerParams(collective_id=cid, has_side_effects=True),
    )


def _body(nd, nt, hidden, norm_gain, head, targets, old_logprob, lengths):
    tok_rows = hidden.shape[0]
    width = hidden.shape[1] * nt
    lanes = 128
    values = hidden.astype(jnp.float32)
    part_sq = jnp.sum(values * values, axis=1)

    ssq_in = jnp.zeros((8, tok_rows), jnp.float32).at[0].set(part_sq)
    tgt_in = jnp.zeros((8, tok_rows), jnp.int32).at[0].set(targets)
    pre = _vmem_call(
        functools.partial(_pre_kernel, nd, nt),
        (jax.ShapeDtypeStruct((nt, 8, tok_rows), jnp.float32),
         jax.ShapeDtypeStruct((nd, 8, tok_rows), jnp.int32)),
        [pltpu.VMEM((nt, 8, tok_rows), jnp.float32),
         pltpu.VMEM((nd, 8, tok_rows), jnp.int32),
         pltpu.SemaphoreType.DMA((nt,)), pltpu.SemaphoreType.DMA((nt,)),
         pltpu.SemaphoreType.DMA((nd,)), pltpu.SemaphoreType.DMA((nd,)),
         pltpu.SemaphoreType.DMA((2,))],
        0,
    )
    q_all, t_all = pre(ssq_in, tgt_in)
    sum_sq = jnp.sum(q_all[:, 0, :], axis=0)
    target_all = t_all[:, 0, :].reshape(nd * tok_rows)

    scaled = lax.rsqrt(sum_sq / width + 1e-06)
    normed = (values * scaled[:, None] * norm_gain[None, :]).astype(jnp.bfloat16)
    vocab_cols = head.shape[1]
    logits = jnp.dot(_gather(normed), head, preferred_element_type=jnp.float32)
    vocab_start = lax.axis_index(("dp", "tensor")) * vocab_cols
    block_top = jnp.max(logits, axis=1)
    block_total = jnp.sum(jnp.exp(logits - block_top[:, None]), axis=1)
    column = vocab_start + jnp.arange(vocab_cols, dtype=jnp.int32)
    hits = column[None, :] == target_all[:, None]
    block_pick = jnp.sum(jnp.where(hits, logits, jnp.float32(0.0)), axis=1)

    stacked = jnp.stack([block_top, block_total, block_pick], axis=0).reshape(3, nd, tok_rows)
    stacked = jnp.transpose(stacked, (1, 0, 2))
    s_in = jnp.concatenate([stacked, jnp.zeros((nd, 5, tok_rows), jnp.float32)], axis=1)
    stats = _vmem_call(
        functools.partial(_stats_kernel, nd, nt),
        jax.ShapeDtypeStruct((nt, nd, 8, tok_rows), jnp.float32),
        [pltpu.VMEM((nd, 8, tok_rows), jnp.float32),
         pltpu.VMEM((nt, nd, 8, tok_rows), jnp.float32),
         pltpu.SemaphoreType.DMA((nd,)), pltpu.SemaphoreType.DMA((nd,)),
         pltpu.SemaphoreType.DMA((nt,)), pltpu.SemaphoreType.DMA((nt,)),
         pltpu.SemaphoreType.DMA((2,))],
        1,
    )(s_in)
    pieces = stats.reshape(nt * nd, 8, tok_rows)
    tops = pieces[:, 0, :]
    top = jnp.max(tops, axis=0)
    total = jnp.sum(pieces[:, 1, :] * jnp.exp(tops - top[None, :]), axis=0)
    picked = jnp.sum(pieces[:, 2, :], axis=0)

    seq_count = lengths.shape[0]
    position = jnp.arange(tok_rows // seq_count, dtype=jnp.int32)
    live = (position[None, :] < lengths[:, None]).reshape(-1).astype(jnp.float32)
    logprob = picked - top - jnp.log(total)
    return (live * logprob, live * (logprob - old_logprob))


def solution(mesh):
    nd = mesh.shape["dp"]
    nt = mesh.shape["tensor"]
    in_specs = (
        P("dp", "tensor"),
        P("tensor"),
        P(None, ("dp", "tensor")),
        P("dp"),
        P("dp"),
        P("dp"),
    )
    out_specs = (P("dp"), P("dp"))
    return jax.shard_map(
        functools.partial(_body, nd, nt), mesh=mesh, in_specs=in_specs, out_specs=out_specs, check_vma=False
    )
```

```python
import functools

import jax
import jax.numpy as jnp
from jax import lax
from jax.experimental import pallas as pl
from jax.experimental.pallas import tpu as pltpu
from jax.sharding import PartitionSpec as P

MESH = pl.DeviceIdType.MESH


def _barrier(nd, nt, d, t):
    barrier = pltpu.get_barrier_semaphore()
    for k in range(1, nd):
        pl.semaphore_signal(barrier, inc=1, device_id=(lax.rem(d + k, nd), t), device_id_type=MESH)
    for k in range(1, nt):
        pl.semaphore_signal(barrier, inc=1, device_id=(d, lax.rem(t + k, nt)), device_id_type=MESH)
    pl.semaphore_wait(barrier, nd - 1 + nt - 1)


def _pre_kernel(nd, nt, ssq_ref, tgt_ref, q_out, t_out, q_buf, t_buf, q_send, q_recv, t_send, t_recv, local):
    d = lax.axis_index("dp")
    t = lax.axis_index("tensor")
    _barrier(nd, nt, d, t)
    own_q = pltpu.make_async_copy(ssq_ref, q_buf.at[t], local.at[0])
    own_t = pltpu.make_async_copy(tgt_ref, t_buf.at[d], local.at[1])
    own_q.start()
    own_t.start()
    sends = []
    for k in range(1, nt):
        c = pltpu.make_async_remote_copy(
            src_ref=ssq_ref, dst_ref=q_buf.at[t], send_sem=q_send.at[k], recv_sem=q_recv.at[t],
            device_id=(d, lax.rem(t + k, nt)), device_id_type=MESH)
        c.start()
        sends.append(c)
    for k in range(1, nd):
        c = pltpu.make_async_remote_copy(
            src_ref=tgt_ref, dst_ref=t_buf.at[d], send_sem=t_send.at[k], recv_sem=t_recv.at[d],
            device_id=(lax.rem(d + k, nd), t), device_id_type=MESH)
        c.start()
        sends.append(c)
    for k in range(1, nt):
        src = lax.rem(t + nt - k, nt)
        pltpu.make_async_remote_copy(
            src_ref=ssq_ref, dst_ref=q_buf.at[src], send_sem=q_send.at[k], recv_sem=q_recv.at[src],
            device_id=(d, src), device_id_type=MESH).wait_recv()
    for k in range(1, nd):
        src = lax.rem(d + nd - k, nd)
        pltpu.make_async_remote_copy(
            src_ref=tgt_ref, dst_ref=t_buf.at[src], send_sem=t_send.at[k], recv_sem=t_recv.at[src],
            device_id=(src, t), device_id_type=MESH).wait_recv()
    for c in sends:
        c.wait_send()
    own_q.wait()
    own_t.wait()
    q_out[...] = q_buf[...]
    t_out[...] = t_buf[...]


def _stats_kernel(nd, nt, s_ref, out_ref, r1, r2, s1_send, s1_recv, s2_send, s2_recv, local):
    d = lax.axis_index("dp")
    t = lax.axis_index("tensor")
    _barrier(nd, nt, d, t)
    own1 = pltpu.make_async_copy(s_ref.at[d], r1.at[d], local.at[0])
    own1.start()
    sends = []
    for k in range(1, nd):
        peer = lax.rem(d + k, nd)
        c = pltpu.make_async_remote_copy(
            src_ref=s_ref.at[peer], dst_ref=r1.at[d], send_sem=s1_send.at[k], recv_sem=s1_recv.at[d],
            device_id=(peer, t), device_id_type=MESH)
        c.start()
        sends.append(c)
    for k in range(1, nd):
        src = lax.rem(d + nd - k, nd)
        pltpu.make_async_remote_copy(
            src_ref=s_ref.at[0], dst_ref=r1.at[src], send_sem=s1_send.at[k], recv_sem=s1_recv.at[src],
            device_id=(src, t), device_id_type=MESH).wait_recv()
    own1.wait()
    own2 = pltpu.make_async_copy(r1, r2.at[t], local.at[1])
    own2.start()
    for k in range(1, nt):
        c = pltpu.make_async_remote_copy(
            src_ref=r1, dst_ref=r2.at[t], send_sem=s2_send.at[k], recv_sem=s2_recv.at[t],
            device_id=(d, lax.rem(t + k, nt)), device_id_type=MESH)
        c.start()
        sends.append(c)
    for k in range(1, nt):
        src = lax.rem(t + nt - k, nt)
        pltpu.make_async_remote_copy(
            src_ref=r1, dst_ref=r2.at[src], send_sem=s2_send.at[k], recv_sem=s2_recv.at[src],
            device_id=(d, src), device_id_type=MESH).wait_recv()
    for c in sends:
        c.wait_send()
    own2.wait()
    out_ref[...] = r2[...]


ORDERS = (("x", "y", "z"), ("y", "z", "x"), ("z", "x", "y"))
PARTS = (48, 48, 32)
RING = 4


def _wrap(v):
    return lax.rem(v + RING, RING)


def _gather_kernel(x_ref, out, ssem, rsem, psend, precv, lsem):
    d = lax.axis_index("dp")
    t = lax.axis_index("tensor")
    cc = lax.rem(t, 2)
    me = {"x": t // 4, "y": lax.rem(d, 4), "z": (lax.rem(t // 2, 2)) * 2 + d // 4}
    cols = x_ref.shape[1]
    half_cols = cols // 2

    def dev(cd):
        return (lax.rem(cd["z"], 2) * 4 + cd["y"], cd["x"] * 4 + (cd["z"] // 2) * 2 + cc)

    def moved(cd, dim, delta):
        cd = dict(cd)
        cd[dim] = _wrap(cd[dim] + delta)
        return cd

    def slab(r, k, center):
        found = [center]
        for dim in ORDERS[r][:k]:
            found = [dict(cd, **{dim: v}) for cd in found for v in range(RING)]
        return found

    offs = (0, PARTS[0], PARTS[0] + PARTS[1])

    def piece(cd, core, r, half):
        row = (lax.rem(cd["z"], 2) * 4 + cd["y"]) * x_ref.shape[0] + offs[r]
        col = (cd["x"] * 4 + (cd["z"] // 2) * 2 + core) * cols
        if half is None:
            return out.at[pl.ds(pl.multiple_of(row, 16), PARTS[r]), pl.ds(pl.multiple_of(col, cols), cols)]
        col = col + half * half_cols
        return out.at[pl.ds(pl.multiple_of(row, 16), PARTS[r]), pl.ds(pl.multiple_of(col, half_cols), half_cols)]

    partner = (d, t + 1 - 2 * cc)
    barrier = pltpu.get_barrier_semaphore()
    for dim in ("x", "y", "z"):
        for delta in (1, -1):
            pl.semaphore_signal(barrier, inc=1, device_id=dev(moved(me, dim, delta)), device_id_type=MESH)
    pl.semaphore_signal(barrier, inc=1, device_id=partner, device_id_type=MESH)
    pl.semaphore_wait(barrier, 7)

    fwd = []

    def to_partner(r, j, cds, half):
        for cd in cds:
            v = piece(cd, cc, r, half)
            pltpu.make_async_remote_copy(
                src_ref=v, dst_ref=v, send_sem=psend.at[r * 13 + j], recv_sem=precv.at[r * 13 + j],
                device_id=partner, device_id_type=MESH).start()
        fwd.append((r * 13 + j, len(cds), r, half))

    own = []
    off = 0
    for r in range(3):
        c = pltpu.make_async_copy(x_ref.at[pl.ds(off, PARTS[r])], piece(me, cc, r, None), lsem.at[r])
        c.start()
        own.append(c)
        off += PARTS[r]
    for r in range(3):
        own[r].wait()
        to_partner(r, 0, [me], None)

    def whole(n, r, half):
        return out.at[pl.ds(0, n * PARTS[r]), pl.ds(0, cols if half is None else half_cols)]

    def recv(group, cds, r, half, src_dev):
        v = whole(len(cds), r, half)
        pltpu.make_async_remote_copy(
            src_ref=v, dst_ref=v, send_sem=ssem.at[group], recv_sem=rsem.at[group],
            device_id=src_dev, device_id_type=MESH).wait_recv()

    sends = []

    def send(group, cds, r, half, dst_dev):
        for cd in cds:
            v = piece(cd, cc, r, half)
            pltpu.make_async_remote_copy(
                src_ref=v, dst_ref=v, send_sem=ssem.at[group], recv_sem=rsem.at[group],
                device_id=dst_dev, device_id_type=MESH).start()
        v = whole(len(cds), r, half)
        sends.append(pltpu.make_async_remote_copy(
            src_ref=v, dst_ref=v, send_sem=ssem.at[group], recv_sem=rsem.at[group],
            device_id=dst_dev, device_id_type=MESH))

    for k in range(3):
        for r in range(3):
            dim = ORDERS[r][k]
            for di, delta in enumerate((1, -1)):
                send((r * 3 + k) * 4 + di, slab(r, k, me), r, None, dev(moved(me, dim, delta)))
        for r in range(3):
            dim = ORDERS[r][k]
            for di, delta in enumerate((1, -1)):
                near = slab(r, k, moved(me, dim, -delta))
                recv((r * 3 + k) * 4 + di, near, r, None, dev(moved(me, dim, -delta)))
                to_partner(r, 1 + 4 * k + di, near, None)
            for di, delta in enumerate((1, -1)):
                near = slab(r, k, moved(me, dim, -delta))
                send((r * 3 + k) * 4 + 2 + di, near, r, di, dev(moved(me, dim, delta)))
        for r in range(3):
            dim = ORDERS[r][k]
            far = slab(r, k, moved(me, dim, 2))
            for di, delta in enumerate((1, -1)):
                recv((r * 3 + k) * 4 + 2 + di, far, r, di, dev(moved(me, dim, -delta)))
                to_partner(r, 3 + 4 * k + di, far, di)
    for c in sends:
        c.wait_send()
    for j, n, r, half in fwd:
        v = whole(n, r, half)
        c = pltpu.make_async_remote_copy(
            src_ref=v, dst_ref=v, send_sem=psend.at[j], recv_sem=precv.at[j],
            device_id=partner, device_id_type=MESH)
        c.wait_send()
        c.wait_recv()


def _gather(normed):
    rows, cols = normed.shape
    return pl.pallas_call(
        _gather_kernel,
        out_shape=jax.ShapeDtypeStruct((2 * RING * rows, RING * 2 * 2 * cols), normed.dtype),
        in_specs=[pl.BlockSpec(memory_space=pltpu.VMEM)],
        out_specs=pl.BlockSpec(memory_space=pl.ANY),
        scratch_shapes=[
            pltpu.SemaphoreType.DMA((36,)), pltpu.SemaphoreType.DMA((36,)),
            pltpu.SemaphoreType.DMA((39,)), pltpu.SemaphoreType.DMA((39,)),
            pltpu.SemaphoreType.DMA((3,)),
        ],
        compiler_params=pltpu.CompilerParams(collective_id=2, has_side_effects=True),
    )(normed)


def _vmem_call(kernel, out_shape, scratch, cid):
    n_out = len(out_shape) if isinstance(out_shape, (tuple, list)) else 1
    out_specs = [pl.BlockSpec(memory_space=pltpu.VMEM)] * n_out
    return pl.pallas_call(
        kernel,
        out_shape=out_shape,
        out_specs=out_specs if n_out > 1 else out_specs[0],
        scratch_shapes=scratch,
        compiler_params=pltpu.CompilerParams(collective_id=cid, has_side_effects=True),
    )


def _body(nd, nt, hidden, norm_gain, head, targets, old_logprob, lengths):
    tok_rows = hidden.shape[0]
    width = hidden.shape[1] * nt
    lanes = 128
    values = hidden.astype(jnp.float32)
    part_sq = jnp.sum(values * values, axis=1)

    ssq_in = jnp.zeros((8, tok_rows), jnp.float32).at[0].set(part_sq)
    tgt_in = jnp.zeros((8, tok_rows), jnp.int32).at[0].set(targets)
    pre = _vmem_call(
        functools.partial(_pre_kernel, nd, nt),
        (jax.ShapeDtypeStruct((nt, 8, tok_rows), jnp.float32),
         jax.ShapeDtypeStruct((nd, 8, tok_rows), jnp.int32)),
        [pltpu.VMEM((nt, 8, tok_rows), jnp.float32),
         pltpu.VMEM((nd, 8, tok_rows), jnp.int32),
         pltpu.SemaphoreType.DMA((nt,)), pltpu.SemaphoreType.DMA((nt,)),
         pltpu.SemaphoreType.DMA((nd,)), pltpu.SemaphoreType.DMA((nd,)),
         pltpu.SemaphoreType.DMA((2,))],
        0,
    )
    q_all, t_all = pre(ssq_in, tgt_in)
    sum_sq = jnp.sum(q_all[:, 0, :], axis=0)
    target_all = t_all[:, 0, :].reshape(nd * tok_rows)

    scaled = lax.rsqrt(sum_sq / width + 1e-06)
    normed = (values * scaled[:, None] * norm_gain[None, :]).astype(jnp.bfloat16)
    vocab_cols = head.shape[1]
    logits = jnp.dot(_gather(normed), head, preferred_element_type=jnp.float32)
    vocab_start = lax.axis_index(("dp", "tensor")) * vocab_cols
    block_top = jnp.max(logits, axis=1)
    block_total = jnp.sum(jnp.exp(logits - block_top[:, None]), axis=1)
    column = vocab_start + jnp.arange(vocab_cols, dtype=jnp.int32)
    hits = column[None, :] == target_all[:, None]
    block_pick = jnp.sum(jnp.where(hits, logits, jnp.float32(0.0)), axis=1)

    stacked = jnp.stack([block_top, block_total, block_pick], axis=0).reshape(3, nd, tok_rows)
    stacked = jnp.transpose(stacked, (1, 0, 2))
    s_in = jnp.concatenate([stacked, jnp.zeros((nd, 5, tok_rows), jnp.float32)], axis=1)
    stats = _vmem_call(
        functools.partial(_stats_kernel, nd, nt),
        jax.ShapeDtypeStruct((nt, nd, 8, tok_rows), jnp.float32),
        [pltpu.VMEM((nd, 8, tok_rows), jnp.float32),
         pltpu.VMEM((nt, nd, 8, tok_rows), jnp.float32),
         pltpu.SemaphoreType.DMA((nd,)), pltpu.SemaphoreType.DMA((nd,)),
         pltpu.SemaphoreType.DMA((nt,)), pltpu.SemaphoreType.DMA((nt,)),
         pltpu.SemaphoreType.DMA((2,))],
        1,
    )(s_in)
    pieces = stats.reshape(nt * nd, 8, tok_rows)
    tops = pieces[:, 0, :]
    top = jnp.max(tops, axis=0)
    total = jnp.sum(pieces[:, 1, :] * jnp.exp(tops - top[None, :]), axis=0)
    picked = jnp.sum(pieces[:, 2, :], axis=0)

    seq_count = lengths.shape[0]
    position = jnp.arange(tok_rows // seq_count, dtype=jnp.int32)
    live = (position[None, :] < lengths[:, None]).reshape(-1).astype(jnp.float32)
    logprob = picked - top - jnp.log(total)
    return (live * logprob, live * (logprob - old_logprob))


def solution(mesh):
    nd = mesh.shape["dp"]
    nt = mesh.shape["tensor"]
    in_specs = (
        P("dp", "tensor"),
        P("tensor"),
        P(None, ("dp", "tensor")),
        P("dp"),
        P("dp"),
        P("dp"),
    )
    out_specs = (P("dp"), P("dp"))
    return jax.shard_map(
        functools.partial(_body, nd, nt), mesh=mesh, in_specs=in_specs, out_specs=out_specs, check_vma=False
    )
```

```python
import functools

import jax
import jax.numpy as jnp
from jax import lax
from jax.experimental import pallas as pl
from jax.experimental.pallas import tpu as pltpu
from jax.sharding import PartitionSpec as P

MESH = pl.DeviceIdType.MESH


def _barrier(nd, nt, d, t):
    barrier = pltpu.get_barrier_semaphore()
    for k in range(1, nd):
        pl.semaphore_signal(barrier, inc=1, device_id=(lax.rem(d + k, nd), t), device_id_type=MESH)
    for k in range(1, nt):
        pl.semaphore_signal(barrier, inc=1, device_id=(d, lax.rem(t + k, nt)), device_id_type=MESH)
    pl.semaphore_wait(barrier, nd - 1 + nt - 1)


def _stats_kernel(nd, nt, s_ref, out_ref, r1, r2, s1_send, s1_recv, s2_send, s2_recv, local):
    d = lax.axis_index("dp")
    t = lax.axis_index("tensor")
    _barrier(nd, nt, d, t)
    own1 = pltpu.make_async_copy(s_ref.at[d], r1.at[d], local.at[0])
    own1.start()
    sends = []
    for k in range(1, nd):
        peer = lax.rem(d + k, nd)
        c = pltpu.make_async_remote_copy(
            src_ref=s_ref.at[peer], dst_ref=r1.at[d], send_sem=s1_send.at[k], recv_sem=s1_recv.at[d],
            device_id=(peer, t), device_id_type=MESH)
        c.start()
        sends.append(c)
    for k in range(1, nd):
        src = lax.rem(d + nd - k, nd)
        pltpu.make_async_remote_copy(
            src_ref=s_ref.at[0], dst_ref=r1.at[src], send_sem=s1_send.at[k], recv_sem=s1_recv.at[src],
            device_id=(src, t), device_id_type=MESH).wait_recv()
    own1.wait()
    own2 = pltpu.make_async_copy(r1, r2.at[t], local.at[1])
    own2.start()
    for k in range(1, nt):
        c = pltpu.make_async_remote_copy(
            src_ref=r1, dst_ref=r2.at[t], send_sem=s2_send.at[k], recv_sem=s2_recv.at[t],
            device_id=(d, lax.rem(t + k, nt)), device_id_type=MESH)
        c.start()
        sends.append(c)
    for k in range(1, nt):
        src = lax.rem(t + nt - k, nt)
        pltpu.make_async_remote_copy(
            src_ref=r1, dst_ref=r2.at[src], send_sem=s2_send.at[k], recv_sem=s2_recv.at[src],
            device_id=(d, src), device_id_type=MESH).wait_recv()
    for c in sends:
        c.wait_send()
    own2.wait()
    out_ref[...] = r2[...]


ORDERS = (("x", "y", "z"), ("y", "z", "x"), ("z", "x", "y"))
PARTS = (48, 48, 32)
RING = 4


def _wrap(v):
    return lax.rem(v + RING, RING)


def _gather_kernel(h_ref, g_ref, ssq_ref, tgt_ref, out, t_out, ssem, rsem, psend, precv, lsem,
                   q_buf, t_buf, x_ref, q_send, q_recv, t_send, t_recv):
    d = lax.axis_index("dp")
    t = lax.axis_index("tensor")
    cc = lax.rem(t, 2)
    me = {"x": t // 4, "y": lax.rem(d, 4), "z": (lax.rem(t // 2, 2)) * 2 + d // 4}
    cols = x_ref.shape[1]
    half_cols = cols // 2

    def dev(cd):
        return (lax.rem(cd["z"], 2) * 4 + cd["y"], cd["x"] * 4 + (cd["z"] // 2) * 2 + cc)

    def moved(cd, dim, delta):
        cd = dict(cd)
        cd[dim] = _wrap(cd[dim] + delta)
        return cd

    def slab(r, k, center):
        found = [center]
        for dim in ORDERS[r][:k]:
            found = [dict(cd, **{dim: v}) for cd in found for v in range(RING)]
        return found

    offs = (0, PARTS[0], PARTS[0] + PARTS[1])

    def piece(cd, core, r, half):
        row = (lax.rem(cd["z"], 2) * 4 + cd["y"]) * x_ref.shape[0] + offs[r]
        col = (cd["x"] * 4 + (cd["z"] // 2) * 2 + core) * cols
        if half is None:
            return out.at[pl.ds(pl.multiple_of(row, 16), PARTS[r]), pl.ds(pl.multiple_of(col, cols), cols)]
        col = col + half * half_cols
        return out.at[pl.ds(pl.multiple_of(row, 16), PARTS[r]), pl.ds(pl.multiple_of(col, half_cols), half_cols)]

    partner = (d, t + 1 - 2 * cc)
    barrier = pltpu.get_barrier_semaphore()
    for dim in ("x", "y", "z"):
        for delta in (1, -1):
            pl.semaphore_signal(barrier, inc=1, device_id=dev(moved(me, dim, delta)), device_id_type=MESH)
    pl.semaphore_signal(barrier, inc=1, device_id=partner, device_id_type=MESH)
    nd, nt = 2 * RING, RING * 2 * 2
    for k in range(1, nd):
        pl.semaphore_signal(barrier, inc=1, device_id=(lax.rem(d + k, nd), t), device_id_type=MESH)
    for k in range(1, nt):
        pl.semaphore_signal(barrier, inc=1, device_id=(d, lax.rem(t + k, nt)), device_id_type=MESH)
    pl.semaphore_wait(barrier, 7 + nd - 1 + nt - 1)

    small = []
    for k in range(1, nt):
        c = pltpu.make_async_remote_copy(
            src_ref=ssq_ref, dst_ref=q_buf.at[t], send_sem=q_send.at[k], recv_sem=q_recv.at[t],
            device_id=(d, lax.rem(t + k, nt)), device_id_type=MESH)
        c.start()
        small.append(c)
    for k in range(1, nd):
        c = pltpu.make_async_remote_copy(
            src_ref=tgt_ref, dst_ref=t_buf.at[d], send_sem=t_send.at[k], recv_sem=t_recv.at[d],
            device_id=(lax.rem(d + k, nd), t), device_id_type=MESH)
        c.start()
        small.append(c)
    own_t = pltpu.make_async_copy(tgt_ref, t_buf.at[d], lsem.at[3])
    own_t.start()
    for k in range(1, nt):
        src = lax.rem(t + nt - k, nt)
        pltpu.make_async_remote_copy(
            src_ref=ssq_ref, dst_ref=q_buf.at[src], send_sem=q_send.at[k], recv_sem=q_recv.at[src],
            device_id=(d, src), device_id_type=MESH).wait_recv()
    ssq = ssq_ref[...]
    for k in range(1, nt):
        ssq = ssq + q_buf[lax.rem(t + k, nt)]
    scale = lax.rsqrt(jnp.transpose(ssq)[:, 0:1] / (nt * cols) + 1e-06)
    x_ref[...] = (h_ref[...].astype(jnp.float32) * scale * g_ref[0:1, :]).astype(x_ref.dtype)

    fwd = []

    def to_partner(r, j, cds, half):
        for cd in cds:
            v = piece(cd, cc, r, half)
            pltpu.make_async_remote_copy(
                src_ref=v, dst_ref=v, send_sem=psend.at[r * 13 + j], recv_sem=precv.at[r * 13 + j],
                device_id=partner, device_id_type=MESH).start()
        fwd.append((r * 13 + j, len(cds), r, half))

    own = []
    off = 0
    for r in range(3):
        c = pltpu.make_async_copy(x_ref.at[pl.ds(off, PARTS[r])], piece(me, cc, r, None), lsem.at[r])
        c.start()
        own.append(c)
        off += PARTS[r]
    for r in range(3):
        own[r].wait()
        to_partner(r, 0, [me], None)

    def whole(n, r, half):
        return out.at[pl.ds(0, n * PARTS[r]), pl.ds(0, cols if half is None else half_cols)]

    def recv(group, cds, r, half, src_dev):
        v = whole(len(cds), r, half)
        pltpu.make_async_remote_copy(
            src_ref=v, dst_ref=v, send_sem=ssem.at[group], recv_sem=rsem.at[group],
            device_id=src_dev, device_id_type=MESH).wait_recv()

    sends = []

    def send(group, cds, r, half, dst_dev):
        for cd in cds:
            v = piece(cd, cc, r, half)
            pltpu.make_async_remote_copy(
                src_ref=v, dst_ref=v, send_sem=ssem.at[group], recv_sem=rsem.at[group],
                device_id=dst_dev, device_id_type=MESH).start()
        v = whole(len(cds), r, half)
        sends.append(pltpu.make_async_remote_copy(
            src_ref=v, dst_ref=v, send_sem=ssem.at[group], recv_sem=rsem.at[group],
            device_id=dst_dev, device_id_type=MESH))

    for k in range(3):
        for r in range(3):
            dim = ORDERS[r][k]
            for di, delta in enumerate((1, -1)):
                send((r * 3 + k) * 4 + di, slab(r, k, me), r, None, dev(moved(me, dim, delta)))
        for r in range(3):
            dim = ORDERS[r][k]
            for di, delta in enumerate((1, -1)):
                near = slab(r, k, moved(me, dim, -delta))
                recv((r * 3 + k) * 4 + di, near, r, None, dev(moved(me, dim, -delta)))
                to_partner(r, 1 + 4 * k + di, near, None)
            for di, delta in enumerate((1, -1)):
                near = slab(r, k, moved(me, dim, -delta))
                send((r * 3 + k) * 4 + 2 + di, near, r, di, dev(moved(me, dim, delta)))
        for r in range(3):
            dim = ORDERS[r][k]
            far = slab(r, k, moved(me, dim, 2))
            for di, delta in enumerate((1, -1)):
                recv((r * 3 + k) * 4 + 2 + di, far, r, di, dev(moved(me, dim, -delta)))
                to_partner(r, 3 + 4 * k + di, far, di)
    for k in range(1, nd):
        src = lax.rem(d + nd - k, nd)
        pltpu.make_async_remote_copy(
            src_ref=tgt_ref, dst_ref=t_buf.at[src], send_sem=t_send.at[k], recv_sem=t_recv.at[src],
            device_id=(src, t), device_id_type=MESH).wait_recv()
    for c in small:
        c.wait_send()
    own_t.wait()
    t_out[...] = t_buf[...]
    for c in sends:
        c.wait_send()
    for j, n, r, half in fwd:
        v = whole(n, r, half)
        c = pltpu.make_async_remote_copy(
            src_ref=v, dst_ref=v, send_sem=psend.at[j], recv_sem=precv.at[j],
            device_id=partner, device_id_type=MESH)
        c.wait_send()
        c.wait_recv()


def _gather(hidden, gain, ssq_in, tgt_in):
    rows, cols = hidden.shape
    nd, nt = 2 * RING, RING * 2 * 2
    return pl.pallas_call(
        _gather_kernel,
        out_shape=(jax.ShapeDtypeStruct((nd * rows, nt * cols), jnp.bfloat16),
                   jax.ShapeDtypeStruct((nd, 8, rows), jnp.int32)),
        in_specs=[pl.BlockSpec(memory_space=pltpu.VMEM)] * 4,
        out_specs=(pl.BlockSpec(memory_space=pl.ANY), pl.BlockSpec(memory_space=pltpu.VMEM)),
        scratch_shapes=[
            pltpu.SemaphoreType.DMA((36,)), pltpu.SemaphoreType.DMA((36,)),
            pltpu.SemaphoreType.DMA((39,)), pltpu.SemaphoreType.DMA((39,)),
            pltpu.SemaphoreType.DMA((4,)),
            pltpu.VMEM((nt, 8, rows), jnp.float32),
            pltpu.VMEM((nd, 8, rows), jnp.int32),
            pltpu.VMEM((rows, cols), jnp.bfloat16),
            pltpu.SemaphoreType.DMA((nt,)), pltpu.SemaphoreType.DMA((nt,)),
            pltpu.SemaphoreType.DMA((nd,)), pltpu.SemaphoreType.DMA((nd,)),
        ],
        compiler_params=pltpu.CompilerParams(collective_id=2, has_side_effects=True),
    )(hidden, gain, ssq_in, tgt_in)


def _vmem_call(kernel, out_shape, scratch, cid):
    n_out = len(out_shape) if isinstance(out_shape, (tuple, list)) else 1
    out_specs = [pl.BlockSpec(memory_space=pltpu.VMEM)] * n_out
    return pl.pallas_call(
        kernel,
        out_shape=out_shape,
        out_specs=out_specs if n_out > 1 else out_specs[0],
        scratch_shapes=scratch,
        compiler_params=pltpu.CompilerParams(collective_id=cid, has_side_effects=True),
    )


def _body(nd, nt, hidden, norm_gain, head, targets, old_logprob, lengths):
    tok_rows = hidden.shape[0]
    values = hidden.astype(jnp.float32)
    part_sq = jnp.sum(values * values, axis=1)

    ssq_in = jnp.zeros((8, tok_rows), jnp.float32).at[0].set(part_sq)
    tgt_in = jnp.zeros((8, tok_rows), jnp.int32).at[0].set(targets)
    gathered, t_all = _gather(hidden, jnp.broadcast_to(norm_gain[None, :], (8, norm_gain.shape[0])), ssq_in, tgt_in)
    target_all = t_all[:, 0, :].reshape(nd * tok_rows)
    logits = jnp.dot(gathered, head, preferred_element_type=jnp.float32)
    vocab_cols = head.shape[1]
    vocab_start = lax.axis_index(("dp", "tensor")) * vocab_cols
    block_top = jnp.max(logits, axis=1)
    block_total = jnp.sum(jnp.exp(logits - block_top[:, None]), axis=1)
    column = vocab_start + jnp.arange(vocab_cols, dtype=jnp.int32)
    hits = column[None, :] == target_all[:, None]
    block_pick = jnp.sum(jnp.where(hits, logits, jnp.float32(0.0)), axis=1)

    stacked = jnp.stack([block_top, block_total, block_pick], axis=0).reshape(3, nd, tok_rows)
    stacked = jnp.transpose(stacked, (1, 0, 2))
    s_in = jnp.concatenate([stacked, jnp.zeros((nd, 5, tok_rows), jnp.float32)], axis=1)
    stats = _vmem_call(
        functools.partial(_stats_kernel, nd, nt),
        jax.ShapeDtypeStruct((nt, nd, 8, tok_rows), jnp.float32),
        [pltpu.VMEM((nd, 8, tok_rows), jnp.float32),
         pltpu.VMEM((nt, nd, 8, tok_rows), jnp.float32),
         pltpu.SemaphoreType.DMA((nd,)), pltpu.SemaphoreType.DMA((nd,)),
         pltpu.SemaphoreType.DMA((nt,)), pltpu.SemaphoreType.DMA((nt,)),
         pltpu.SemaphoreType.DMA((2,))],
        1,
    )(s_in)
    pieces = stats.reshape(nt * nd, 8, tok_rows)
    tops = pieces[:, 0, :]
    top = jnp.max(tops, axis=0)
    total = jnp.sum(pieces[:, 1, :] * jnp.exp(tops - top[None, :]), axis=0)
    picked = jnp.sum(pieces[:, 2, :], axis=0)

    seq_count = lengths.shape[0]
    position = jnp.arange(tok_rows // seq_count, dtype=jnp.int32)
    live = (position[None, :] < lengths[:, None]).reshape(-1).astype(jnp.float32)
    logprob = picked - top - jnp.log(total)
    return (live * logprob, live * (logprob - old_logprob))


def solution(mesh):
    nd = mesh.shape["dp"]
    nt = mesh.shape["tensor"]
    in_specs = (
        P("dp", "tensor"),
        P("tensor"),
        P(None, ("dp", "tensor")),
        P("dp"),
        P("dp"),
        P("dp"),
    )
    out_specs = (P("dp"), P("dp"))
    return jax.shard_map(
        functools.partial(_body, nd, nt), mesh=mesh, in_specs=in_specs, out_specs=out_specs, check_vma=False
    )
```

```python
import functools

import jax
import jax.numpy as jnp
from jax import lax
from jax.experimental import pallas as pl
from jax.experimental.pallas import tpu as pltpu
from jax.sharding import PartitionSpec as P

MESH = pl.DeviceIdType.MESH


def _barrier(nd, nt, d, t):
    barrier = pltpu.get_barrier_semaphore()
    for k in range(1, nd):
        pl.semaphore_signal(barrier, inc=1, device_id=(lax.rem(d + k, nd), t), device_id_type=MESH)
    for k in range(1, nt):
        pl.semaphore_signal(barrier, inc=1, device_id=(d, lax.rem(t + k, nt)), device_id_type=MESH)
    pl.semaphore_wait(barrier, nd - 1 + nt - 1)


def _stats_kernel(nd, nt, s_ref, out_ref, r1, r2, s1_send, s1_recv, s2_send, s2_recv, local):
    d = lax.axis_index("dp")
    t = lax.axis_index("tensor")
    _barrier(nd, nt, d, t)
    own1 = pltpu.make_async_copy(s_ref.at[d], r1.at[d], local.at[0])
    own1.start()
    sends = []
    for k in range(1, nd):
        peer = lax.rem(d + k, nd)
        c = pltpu.make_async_remote_copy(
            src_ref=s_ref.at[peer], dst_ref=r1.at[d], send_sem=s1_send.at[k], recv_sem=s1_recv.at[d],
            device_id=(peer, t), device_id_type=MESH)
        c.start()
        sends.append(c)
    for k in range(1, nd):
        src = lax.rem(d + nd - k, nd)
        pltpu.make_async_remote_copy(
            src_ref=s_ref.at[0], dst_ref=r1.at[src], send_sem=s1_send.at[k], recv_sem=s1_recv.at[src],
            device_id=(src, t), device_id_type=MESH).wait_recv()
    own1.wait()
    own2 = pltpu.make_async_copy(r1, r2.at[t], local.at[1])
    own2.start()
    for k in range(1, nt):
        c = pltpu.make_async_remote_copy(
            src_ref=r1, dst_ref=r2.at[t], send_sem=s2_send.at[k], recv_sem=s2_recv.at[t],
            device_id=(d, lax.rem(t + k, nt)), device_id_type=MESH)
        c.start()
        sends.append(c)
    for k in range(1, nt):
        src = lax.rem(t + nt - k, nt)
        pltpu.make_async_remote_copy(
            src_ref=r1, dst_ref=r2.at[src], send_sem=s2_send.at[k], recv_sem=s2_recv.at[src],
            device_id=(d, src), device_id_type=MESH).wait_recv()
    for c in sends:
        c.wait_send()
    own2.wait()
    out_ref[...] = r2[...]


ORDERS = (("x", "y", "z"), ("y", "z", "x"), ("z", "x", "y"))
PARTS = (48, 48, 32)
RING = 4


def _wrap(v):
    return lax.rem(v + RING, RING)


def _gather_kernel(h_ref, g_ref, ssq_ref, tgt_ref, out, t_out, ssem, rsem, psend, precv, lsem,
                   q_buf, t_buf, x_ref, q_send, q_recv, t_send, t_recv):
    d = lax.axis_index("dp")
    t = lax.axis_index("tensor")
    cc = lax.rem(t, 2)
    me = {"x": t // 4, "y": lax.rem(d, 4), "z": (lax.rem(t // 2, 2)) * 2 + d // 4}
    cols = x_ref.shape[1]
    half_cols = cols // 2

    def dev(cd):
        return (lax.rem(cd["z"], 2) * 4 + cd["y"], cd["x"] * 4 + (cd["z"] // 2) * 2 + cc)

    def moved(cd, dim, delta):
        cd = dict(cd)
        cd[dim] = _wrap(cd[dim] + delta)
        return cd

    def slab(r, k, center):
        found = [center]
        for dim in ORDERS[r][:k]:
            found = [dict(cd, **{dim: v}) for cd in found for v in range(RING)]
        return found

    offs = (0, PARTS[0], PARTS[0] + PARTS[1])

    def piece(cd, core, r, half):
        row = (lax.rem(cd["z"], 2) * 4 + cd["y"]) * x_ref.shape[0] + offs[r]
        col = (cd["x"] * 4 + (cd["z"] // 2) * 2 + core) * cols
        if half is None:
            return out.at[pl.ds(pl.multiple_of(row, 16), PARTS[r]), pl.ds(pl.multiple_of(col, cols), cols)]
        col = col + half * half_cols
        return out.at[pl.ds(pl.multiple_of(row, 16), PARTS[r]), pl.ds(pl.multiple_of(col, half_cols), half_cols)]

    partner = (d, t + 1 - 2 * cc)
    barrier = pltpu.get_barrier_semaphore()
    for dim in ("x", "y", "z"):
        for delta in (1, -1):
            pl.semaphore_signal(barrier, inc=1, device_id=dev(moved(me, dim, delta)), device_id_type=MESH)
    pl.semaphore_signal(barrier, inc=1, device_id=partner, device_id_type=MESH)
    nd, nt = 2 * RING, RING * 2 * 2
    for k in range(1, nd):
        pl.semaphore_signal(barrier, inc=1, device_id=(lax.rem(d + k, nd), t), device_id_type=MESH)
    for k in range(1, nt):
        pl.semaphore_signal(barrier, inc=1, device_id=(d, lax.rem(t + k, nt)), device_id_type=MESH)
    pl.semaphore_wait(barrier, 7 + nd - 1 + nt - 1)

    small = []
    for k in range(1, nt):
        c = pltpu.make_async_remote_copy(
            src_ref=ssq_ref, dst_ref=q_buf.at[t], send_sem=q_send.at[k], recv_sem=q_recv.at[t],
            device_id=(d, lax.rem(t + k, nt)), device_id_type=MESH)
        c.start()
        small.append(c)
    for k in range(1, nd):
        c = pltpu.make_async_remote_copy(
            src_ref=tgt_ref, dst_ref=t_buf.at[d], send_sem=t_send.at[k], recv_sem=t_recv.at[d],
            device_id=(lax.rem(d + k, nd), t), device_id_type=MESH)
        c.start()
        small.append(c)
    own_t = pltpu.make_async_copy(tgt_ref, t_buf.at[d], lsem.at[3])
    own_t.start()
    for k in range(1, nt):
        src = lax.rem(t + nt - k, nt)
        pltpu.make_async_remote_copy(
            src_ref=ssq_ref, dst_ref=q_buf.at[src], send_sem=q_send.at[k], recv_sem=q_recv.at[src],
            device_id=(d, src), device_id_type=MESH).wait_recv()
    ssq = ssq_ref[...]
    for k in range(1, nt):
        ssq = ssq + q_buf[lax.rem(t + k, nt)]
    scale = lax.rsqrt(jnp.transpose(ssq)[:, 0:1] / (nt * cols) + 1e-06)
    x_ref[...] = (h_ref[...].astype(jnp.float32) * scale * g_ref[0:1, :]).astype(x_ref.dtype)

    fwd = []

    def to_partner(r, j, cds, half):
        for cd in cds:
            v = piece(cd, cc, r, half)
            pltpu.make_async_remote_copy(
                src_ref=v, dst_ref=v, send_sem=psend.at[r * 13 + j], recv_sem=precv.at[r * 13 + j],
                device_id=partner, device_id_type=MESH).start()
        fwd.append((r * 13 + j, len(cds), r, half))

    own = []
    off = 0
    for r in range(3):
        c = pltpu.make_async_copy(x_ref.at[pl.ds(off, PARTS[r])], piece(me, cc, r, None), lsem.at[r])
        c.start()
        own.append(c)
        off += PARTS[r]
    for r in range(3):
        own[r].wait()
        to_partner(r, 0, [me], None)

    def whole(n, r, half):
        return out.at[pl.ds(0, n * PARTS[r]), pl.ds(0, cols if half is None else half_cols)]

    def recv(group, cds, r, half, src_dev):
        v = whole(len(cds), r, half)
        pltpu.make_async_remote_copy(
            src_ref=v, dst_ref=v, send_sem=ssem.at[group], recv_sem=rsem.at[group],
            device_id=src_dev, device_id_type=MESH).wait_recv()

    sends = []

    def send(group, cds, r, half, dst_dev):
        for cd in cds:
            v = piece(cd, cc, r, half)
            pltpu.make_async_remote_copy(
                src_ref=v, dst_ref=v, send_sem=ssem.at[group], recv_sem=rsem.at[group],
                device_id=dst_dev, device_id_type=MESH).start()
        v = whole(len(cds), r, half)
        sends.append(pltpu.make_async_remote_copy(
            src_ref=v, dst_ref=v, send_sem=ssem.at[group], recv_sem=rsem.at[group],
            device_id=dst_dev, device_id_type=MESH))

    for k in range(3):
        for r in range(3):
            dim = ORDERS[r][k]
            for di, delta in enumerate((1, -1)):
                send((r * 3 + k) * 4 + di, slab(r, k, me), r, None, dev(moved(me, dim, delta)))
        for r in range(3):
            dim = ORDERS[r][k]
            for di, delta in enumerate((1, -1)):
                near = slab(r, k, moved(me, dim, -delta))
                recv((r * 3 + k) * 4 + di, near, r, None, dev(moved(me, dim, -delta)))
                to_partner(r, 1 + 4 * k + di, near, None)
            for di, delta in enumerate((1, -1)):
                near = slab(r, k, moved(me, dim, -delta))
                send((r * 3 + k) * 4 + 2 + di, near, r, di, dev(moved(me, dim, delta)))
        for r in range(3):
            dim = ORDERS[r][k]
            far = slab(r, k, moved(me, dim, 2))
            for di, delta in enumerate((1, -1)):
                recv((r * 3 + k) * 4 + 2 + di, far, r, di, dev(moved(me, dim, -delta)))
                to_partner(r, 3 + 4 * k + di, far, di)
    for k in range(1, nd):
        src = lax.rem(d + nd - k, nd)
        pltpu.make_async_remote_copy(
            src_ref=tgt_ref, dst_ref=t_buf.at[src], send_sem=t_send.at[k], recv_sem=t_recv.at[src],
            device_id=(src, t), device_id_type=MESH).wait_recv()
    for c in small:
        c.wait_send()
    own_t.wait()
    t_out[...] = t_buf[...]
    for c in sends:
        c.wait_send()
    for j, n, r, half in fwd:
        v = whole(n, r, half)
        c = pltpu.make_async_remote_copy(
            src_ref=v, dst_ref=v, send_sem=psend.at[j], recv_sem=precv.at[j],
            device_id=partner, device_id_type=MESH)
        c.wait_send()
        c.wait_recv()


def _gather(hidden, gain, ssq_in, tgt_in):
    rows, cols = hidden.shape
    nd, nt = 2 * RING, RING * 2 * 2
    return pl.pallas_call(
        _gather_kernel,
        out_shape=(jax.ShapeDtypeStruct((nd * rows, nt * cols), jnp.bfloat16),
                   jax.ShapeDtypeStruct((nd, 8, rows), jnp.int32)),
        in_specs=[pl.BlockSpec(memory_space=pltpu.VMEM)] * 4,
        out_specs=(pl.BlockSpec(memory_space=pl.ANY), pl.BlockSpec(memory_space=pltpu.VMEM)),
        scratch_shapes=[
            pltpu.SemaphoreType.DMA((36,)), pltpu.SemaphoreType.DMA((36,)),
            pltpu.SemaphoreType.DMA((39,)), pltpu.SemaphoreType.DMA((39,)),
            pltpu.SemaphoreType.DMA((4,)),
            pltpu.VMEM((nt, 8, rows), jnp.float32),
            pltpu.VMEM((nd, 8, rows), jnp.int32),
            pltpu.VMEM((rows, cols), jnp.bfloat16),
            pltpu.SemaphoreType.DMA((nt,)), pltpu.SemaphoreType.DMA((nt,)),
            pltpu.SemaphoreType.DMA((nd,)), pltpu.SemaphoreType.DMA((nd,)),
        ],
        compiler_params=pltpu.CompilerParams(collective_id=2, has_side_effects=True),
    )(hidden, gain, ssq_in, tgt_in)


def _vmem_call(kernel, out_shape, scratch, cid):
    n_out = len(out_shape) if isinstance(out_shape, (tuple, list)) else 1
    out_specs = [pl.BlockSpec(memory_space=pltpu.VMEM)] * n_out
    return pl.pallas_call(
        kernel,
        out_shape=out_shape,
        out_specs=out_specs if n_out > 1 else out_specs[0],
        scratch_shapes=scratch,
        compiler_params=pltpu.CompilerParams(collective_id=cid, has_side_effects=True),
    )


def _body(nd, nt, hidden, norm_gain, head, targets, old_logprob, lengths):
    tok_rows = hidden.shape[0]
    values = hidden.astype(jnp.float32)
    part_sq = jnp.sum(values * values, axis=1)

    ssq_in = jnp.broadcast_to(part_sq[None, :], (8, tok_rows))
    tgt_in = jnp.broadcast_to(targets[None, :], (8, tok_rows))
    gathered, t_all = _gather(hidden, norm_gain[None, :], ssq_in, tgt_in)
    target_all = t_all[:, 0, :].reshape(nd * tok_rows)
    logits = jnp.dot(gathered, head, preferred_element_type=jnp.float32)
    vocab_cols = head.shape[1]
    vocab_start = lax.axis_index(("dp", "tensor")) * vocab_cols
    block_top = jnp.max(logits, axis=1)
    block_total = jnp.sum(jnp.exp(logits - block_top[:, None]), axis=1)
    column = vocab_start + jnp.arange(vocab_cols, dtype=jnp.int32)
    hits = column[None, :] == target_all[:, None]
    block_pick = jnp.sum(jnp.where(hits, logits, jnp.float32(0.0)), axis=1)

    stacked = jnp.stack([block_top, block_total, block_pick] + [block_top] * 5, axis=0).reshape(8, nd, tok_rows)
    s_in = jnp.transpose(stacked, (1, 0, 2))
    stats = _vmem_call(
        functools.partial(_stats_kernel, nd, nt),
        jax.ShapeDtypeStruct((nt, nd, 8, tok_rows), jnp.float32),
        [pltpu.VMEM((nd, 8, tok_rows), jnp.float32),
         pltpu.VMEM((nt, nd, 8, tok_rows), jnp.float32),
         pltpu.SemaphoreType.DMA((nd,)), pltpu.SemaphoreType.DMA((nd,)),
         pltpu.SemaphoreType.DMA((nt,)), pltpu.SemaphoreType.DMA((nt,)),
         pltpu.SemaphoreType.DMA((2,))],
        1,
    )(s_in)
    pieces = stats.reshape(nt * nd, 8, tok_rows)
    tops = pieces[:, 0, :]
    top = jnp.max(tops, axis=0)
    total = jnp.sum(pieces[:, 1, :] * jnp.exp(tops - top[None, :]), axis=0)
    picked = jnp.sum(pieces[:, 2, :], axis=0)

    seq_count = lengths.shape[0]
    position = jnp.arange(tok_rows // seq_count, dtype=jnp.int32)
    live = (position[None, :] < lengths[:, None]).reshape(-1).astype(jnp.float32)
    logprob = picked - top - jnp.log(total)
    return (live * logprob, live * (logprob - old_logprob))


def solution(mesh):
    nd = mesh.shape["dp"]
    nt = mesh.shape["tensor"]
    in_specs = (
        P("dp", "tensor"),
        P("tensor"),
        P(None, ("dp", "tensor")),
        P("dp"),
        P("dp"),
        P("dp"),
    )
    out_specs = (P("dp"), P("dp"))
    return jax.shard_map(
        functools.partial(_body, nd, nt), mesh=mesh, in_specs=in_specs, out_specs=out_specs, check_vma=False
    )
```

```python
import functools

import jax
import jax.numpy as jnp
from jax import lax
from jax.experimental import pallas as pl
from jax.experimental.pallas import tpu as pltpu
from jax.sharding import PartitionSpec as P

MESH = pl.DeviceIdType.MESH


def _barrier(nd, nt, d, t):
    barrier = pltpu.get_barrier_semaphore()
    for k in range(1, nd):
        pl.semaphore_signal(barrier, inc=1, device_id=(lax.rem(d + k, nd), t), device_id_type=MESH)
    for k in range(1, nt):
        pl.semaphore_signal(barrier, inc=1, device_id=(d, lax.rem(t + k, nt)), device_id_type=MESH)
    pl.semaphore_wait(barrier, nd - 1 + nt - 1)


def _stats_kernel(nd, nt, s_ref, out_ref, r1, r2, s1_send, s1_recv, s2_send, s2_recv, local):
    d = lax.axis_index("dp")
    t = lax.axis_index("tensor")
    _barrier(nd, nt, d, t)
    own1 = pltpu.make_async_copy(s_ref.at[d], r1.at[d], local.at[0])
    own1.start()
    sends = []
    for k in range(1, nd):
        peer = lax.rem(d + k, nd)
        c = pltpu.make_async_remote_copy(
            src_ref=s_ref.at[peer], dst_ref=r1.at[d], send_sem=s1_send.at[k], recv_sem=s1_recv.at[d],
            device_id=(peer, t), device_id_type=MESH)
        c.start()
        sends.append(c)
    for k in range(1, nd):
        src = lax.rem(d + nd - k, nd)
        pltpu.make_async_remote_copy(
            src_ref=s_ref.at[0], dst_ref=r1.at[src], send_sem=s1_send.at[k], recv_sem=s1_recv.at[src],
            device_id=(src, t), device_id_type=MESH).wait_recv()
    own1.wait()
    own2 = pltpu.make_async_copy(r1, r2.at[t], local.at[1])
    own2.start()
    for k in range(1, nt):
        c = pltpu.make_async_remote_copy(
            src_ref=r1, dst_ref=r2.at[t], send_sem=s2_send.at[k], recv_sem=s2_recv.at[t],
            device_id=(d, lax.rem(t + k, nt)), device_id_type=MESH)
        c.start()
        sends.append(c)
    for k in range(1, nt):
        src = lax.rem(t + nt - k, nt)
        pltpu.make_async_remote_copy(
            src_ref=r1, dst_ref=r2.at[src], send_sem=s2_send.at[k], recv_sem=s2_recv.at[src],
            device_id=(d, src), device_id_type=MESH).wait_recv()
    for c in sends:
        c.wait_send()
    own2.wait()
    out_ref[...] = r2[...]


ORDERS = (("x", "y", "z"), ("y", "z", "x"), ("z", "x", "y"))
PARTS = (48, 48, 32)
RING = 4


def _wrap(v):
    return lax.rem(v + RING, RING)


def _gather_kernel(h_ref, g_ref, ssq_ref, tgt_ref, out, t_out, ssem, rsem, psend, precv, lsem,
                   q_buf, t_buf, x_ref, q_send, q_recv, t_send, t_recv):
    d = lax.axis_index("dp")
    t = lax.axis_index("tensor")
    cc = lax.rem(t, 2)
    me = {"x": t // 4, "y": lax.rem(d, 4), "z": (lax.rem(t // 2, 2)) * 2 + d // 4}
    cols = x_ref.shape[1]
    half_cols = cols // 2

    def dev(cd):
        return (lax.rem(cd["z"], 2) * 4 + cd["y"], cd["x"] * 4 + (cd["z"] // 2) * 2 + cc)

    def moved(cd, dim, delta):
        cd = dict(cd)
        cd[dim] = _wrap(cd[dim] + delta)
        return cd

    def slab(r, k, center):
        found = [center]
        for dim in ORDERS[r][:k]:
            found = [dict(cd, **{dim: v}) for cd in found for v in range(RING)]
        return found

    offs = (0, PARTS[0], PARTS[0] + PARTS[1])

    def piece(cd, core, r, half):
        row = (lax.rem(cd["z"], 2) * 4 + cd["y"]) * x_ref.shape[0] + offs[r]
        col = (cd["x"] * 4 + (cd["z"] // 2) * 2 + core) * cols
        if half is None:
            return out.at[pl.ds(pl.multiple_of(row, 16), PARTS[r]), pl.ds(pl.multiple_of(col, cols), cols)]
        col = col + half * half_cols
        return out.at[pl.ds(pl.multiple_of(row, 16), PARTS[r]), pl.ds(pl.multiple_of(col, half_cols), half_cols)]

    partner = (d, t + 1 - 2 * cc)
    barrier = pltpu.get_barrier_semaphore()
    for dim in ("x", "y", "z"):
        for delta in (1, -1):
            pl.semaphore_signal(barrier, inc=1, device_id=dev(moved(me, dim, delta)), device_id_type=MESH)
    pl.semaphore_signal(barrier, inc=1, device_id=partner, device_id_type=MESH)
    nd, nt = 2 * RING, RING * 2 * 2
    for k in range(1, nd):
        pl.semaphore_signal(barrier, inc=1, device_id=(lax.rem(d + k, nd), t), device_id_type=MESH)
    for k in range(1, nt):
        pl.semaphore_signal(barrier, inc=1, device_id=(d, lax.rem(t + k, nt)), device_id_type=MESH)
    pl.semaphore_wait(barrier, 7 + nd - 1 + nt - 1)

    small = []
    for k in range(1, nt):
        c = pltpu.make_async_remote_copy(
            src_ref=ssq_ref, dst_ref=q_buf.at[t], send_sem=q_send.at[k], recv_sem=q_recv.at[t],
            device_id=(d, lax.rem(t + k, nt)), device_id_type=MESH)
        c.start()
        small.append(c)
    for k in range(1, nd):
        c = pltpu.make_async_remote_copy(
            src_ref=tgt_ref, dst_ref=t_buf.at[d], send_sem=t_send.at[k], recv_sem=t_recv.at[d],
            device_id=(lax.rem(d + k, nd), t), device_id_type=MESH)
        c.start()
        small.append(c)
    own_t = pltpu.make_async_copy(tgt_ref, t_buf.at[d], lsem.at[3])
    own_t.start()
    for k in range(1, nt):
        src = lax.rem(t + nt - k, nt)
        pltpu.make_async_remote_copy(
            src_ref=ssq_ref, dst_ref=q_buf.at[src], send_sem=q_send.at[k], recv_sem=q_recv.at[src],
            device_id=(d, src), device_id_type=MESH).wait_recv()
    ssq = ssq_ref[...]
    for k in range(1, nt):
        ssq = ssq + q_buf[lax.rem(t + k, nt)]
    scale = lax.rsqrt(jnp.transpose(ssq)[:, 0:1] / (nt * cols) + 1e-06)
    x_ref[...] = (h_ref[...].astype(jnp.float32) * scale * g_ref[0:1, :]).astype(x_ref.dtype)

    fwd = []

    def to_partner(r, j, cds, half):
        for cd in cds:
            v = piece(cd, cc, r, half)
            pltpu.make_async_remote_copy(
                src_ref=v, dst_ref=v, send_sem=psend.at[r * 13 + j], recv_sem=precv.at[r * 13 + j],
                device_id=partner, device_id_type=MESH).start()
        fwd.append((r * 13 + j, len(cds), r, half))

    own = []
    off = 0
    for r in range(3):
        c = pltpu.make_async_copy(x_ref.at[pl.ds(off, PARTS[r])], piece(me, cc, r, None), lsem.at[r])
        c.start()
        own.append(c)
        off += PARTS[r]
    for r in range(3):
        own[r].wait()
        to_partner(r, 0, [me], None)

    def whole(n, r, half):
        return out.at[pl.ds(0, n * PARTS[r]), pl.ds(0, cols if half is None else half_cols)]

    def recv(group, cds, r, half, src_dev):
        v = whole(len(cds), r, half)
        pltpu.make_async_remote_copy(
            src_ref=v, dst_ref=v, send_sem=ssem.at[group], recv_sem=rsem.at[group],
            device_id=src_dev, device_id_type=MESH).wait_recv()

    sends = []

    def send(group, cds, r, half, dst_dev):
        for cd in cds:
            v = piece(cd, cc, r, half)
            pltpu.make_async_remote_copy(
                src_ref=v, dst_ref=v, send_sem=ssem.at[group], recv_sem=rsem.at[group],
                device_id=dst_dev, device_id_type=MESH).start()
        v = whole(len(cds), r, half)
        sends.append(pltpu.make_async_remote_copy(
            src_ref=v, dst_ref=v, send_sem=ssem.at[group], recv_sem=rsem.at[group],
            device_id=dst_dev, device_id_type=MESH))

    later = []
    for k in range(3):
        for r in range(3):
            dim = ORDERS[r][k]
            for di, delta in enumerate((1, -1)):
                send((r * 3 + k) * 4 + di, slab(r, k, me), r, None, dev(moved(me, dim, delta)))
        for args in later:
            to_partner(*args)
        later = []
        for r in range(3):
            dim = ORDERS[r][k]
            for di, delta in enumerate((1, -1)):
                near = slab(r, k, moved(me, dim, -delta))
                recv((r * 3 + k) * 4 + di, near, r, None, dev(moved(me, dim, -delta)))
            for di, delta in enumerate((1, -1)):
                near = slab(r, k, moved(me, dim, -delta))
                send((r * 3 + k) * 4 + 2 + di, near, r, di, dev(moved(me, dim, delta)))
            for di, delta in enumerate((1, -1)):
                to_partner(r, 1 + 4 * k + di, slab(r, k, moved(me, dim, -delta)), None)
        for r in range(3):
            dim = ORDERS[r][k]
            far = slab(r, k, moved(me, dim, 2))
            for di, delta in enumerate((1, -1)):
                recv((r * 3 + k) * 4 + 2 + di, far, r, di, dev(moved(me, dim, -delta)))
                later.append((r, 3 + 4 * k + di, far, di))
    for args in later:
        to_partner(*args)
    for k in range(1, nd):
        src = lax.rem(d + nd - k, nd)
        pltpu.make_async_remote_copy(
            src_ref=tgt_ref, dst_ref=t_buf.at[src], send_sem=t_send.at[k], recv_sem=t_recv.at[src],
            device_id=(src, t), device_id_type=MESH).wait_recv()
    for c in small:
        c.wait_send()
    own_t.wait()
    t_out[...] = t_buf[...]
    for c in sends:
        c.wait_send()
    for j, n, r, half in fwd:
        v = whole(n, r, half)
        c = pltpu.make_async_remote_copy(
            src_ref=v, dst_ref=v, send_sem=psend.at[j], recv_sem=precv.at[j],
            device_id=partner, device_id_type=MESH)
        c.wait_send()
        c.wait_recv()


def _gather(hidden, gain, ssq_in, tgt_in):
    rows, cols = hidden.shape
    nd, nt = 2 * RING, RING * 2 * 2
    return pl.pallas_call(
        _gather_kernel,
        out_shape=(jax.ShapeDtypeStruct((nd * rows, nt * cols), jnp.bfloat16),
                   jax.ShapeDtypeStruct((nd, 8, rows), jnp.int32)),
        in_specs=[pl.BlockSpec(memory_space=pltpu.VMEM)] * 4,
        out_specs=(pl.BlockSpec(memory_space=pl.ANY), pl.BlockSpec(memory_space=pltpu.VMEM)),
        scratch_shapes=[
            pltpu.SemaphoreType.DMA((36,)), pltpu.SemaphoreType.DMA((36,)),
            pltpu.SemaphoreType.DMA((39,)), pltpu.SemaphoreType.DMA((39,)),
            pltpu.SemaphoreType.DMA((4,)),
            pltpu.VMEM((nt, 8, rows), jnp.float32),
            pltpu.VMEM((nd, 8, rows), jnp.int32),
            pltpu.VMEM((rows, cols), jnp.bfloat16),
            pltpu.SemaphoreType.DMA((nt,)), pltpu.SemaphoreType.DMA((nt,)),
            pltpu.SemaphoreType.DMA((nd,)), pltpu.SemaphoreType.DMA((nd,)),
        ],
        compiler_params=pltpu.CompilerParams(collective_id=2, has_side_effects=True),
    )(hidden, gain, ssq_in, tgt_in)


def _vmem_call(kernel, out_shape, scratch, cid):
    n_out = len(out_shape) if isinstance(out_shape, (tuple, list)) else 1
    out_specs = [pl.BlockSpec(memory_space=pltpu.VMEM)] * n_out
    return pl.pallas_call(
        kernel,
        out_shape=out_shape,
        out_specs=out_specs if n_out > 1 else out_specs[0],
        scratch_shapes=scratch,
        compiler_params=pltpu.CompilerParams(collective_id=cid, has_side_effects=True),
    )


def _body(nd, nt, hidden, norm_gain, head, targets, old_logprob, lengths):
    tok_rows = hidden.shape[0]
    values = hidden.astype(jnp.float32)
    part_sq = jnp.sum(values * values, axis=1)

    ssq_in = jnp.broadcast_to(part_sq[None, :], (8, tok_rows))
    tgt_in = jnp.broadcast_to(targets[None, :], (8, tok_rows))
    gathered, t_all = _gather(hidden, norm_gain[None, :], ssq_in, tgt_in)
    target_all = t_all[:, 0, :].reshape(nd * tok_rows)
    logits = jnp.dot(gathered, head, preferred_element_type=jnp.float32)
    vocab_cols = head.shape[1]
    vocab_start = lax.axis_index(("dp", "tensor")) * vocab_cols
    block_top = jnp.max(logits, axis=1)
    block_total = jnp.sum(jnp.exp(logits - block_top[:, None]), axis=1)
    column = vocab_start + jnp.arange(vocab_cols, dtype=jnp.int32)
    hits = column[None, :] == target_all[:, None]
    block_pick = jnp.sum(jnp.where(hits, logits, jnp.float32(0.0)), axis=1)

    stacked = jnp.stack([block_top, block_total, block_pick] + [block_top] * 5, axis=0).reshape(8, nd, tok_rows)
    s_in = jnp.transpose(stacked, (1, 0, 2))
    stats = _vmem_call(
        functools.partial(_stats_kernel, nd, nt),
        jax.ShapeDtypeStruct((nt, nd, 8, tok_rows), jnp.float32),
        [pltpu.VMEM((nd, 8, tok_rows), jnp.float32),
         pltpu.VMEM((nt, nd, 8, tok_rows), jnp.float32),
         pltpu.SemaphoreType.DMA((nd,)), pltpu.SemaphoreType.DMA((nd,)),
         pltpu.SemaphoreType.DMA((nt,)), pltpu.SemaphoreType.DMA((nt,)),
         pltpu.SemaphoreType.DMA((2,))],
        1,
    )(s_in)
    pieces = stats.reshape(nt * nd, 8, tok_rows)
    tops = pieces[:, 0, :]
    top = jnp.max(tops, axis=0)
    total = jnp.sum(pieces[:, 1, :] * jnp.exp(tops - top[None, :]), axis=0)
    picked = jnp.sum(pieces[:, 2, :], axis=0)

    seq_count = lengths.shape[0]
    position = jnp.arange(tok_rows // seq_count, dtype=jnp.int32)
    live = (position[None, :] < lengths[:, None]).reshape(-1).astype(jnp.float32)
    logprob = picked - top - jnp.log(total)
    return (live * logprob, live * (logprob - old_logprob))


def solution(mesh):
    nd = mesh.shape["dp"]
    nt = mesh.shape["tensor"]
    in_specs = (
        P("dp", "tensor"),
        P("tensor"),
        P(None, ("dp", "tensor")),
        P("dp"),
        P("dp"),
        P("dp"),
    )
    out_specs = (P("dp"), P("dp"))
    return jax.shard_map(
        functools.partial(_body, nd, nt), mesh=mesh, in_specs=in_specs, out_specs=out_specs, check_vma=False
    )
```

```python
import functools

import jax
import jax.numpy as jnp
from jax import lax
from jax.experimental import pallas as pl
from jax.experimental.pallas import tpu as pltpu
from jax.sharding import PartitionSpec as P

MESH = pl.DeviceIdType.MESH


def _barrier(nd, nt, d, t):
    barrier = pltpu.get_barrier_semaphore()
    for k in range(1, nd):
        pl.semaphore_signal(barrier, inc=1, device_id=(lax.rem(d + k, nd), t), device_id_type=MESH)
    for k in range(1, nt):
        pl.semaphore_signal(barrier, inc=1, device_id=(d, lax.rem(t + k, nt)), device_id_type=MESH)
    pl.semaphore_wait(barrier, nd - 1 + nt - 1)


def _stats_kernel(nd, nt, s_ref, out_ref, r1, r2, s1_send, s1_recv, s2_send, s2_recv, local):
    d = lax.axis_index("dp")
    t = lax.axis_index("tensor")
    _barrier(nd, nt, d, t)
    own1 = pltpu.make_async_copy(s_ref.at[d], r1.at[d], local.at[0])
    own1.start()
    sends = []
    for k in range(1, nd):
        peer = lax.rem(d + k, nd)
        c = pltpu.make_async_remote_copy(
            src_ref=s_ref.at[peer], dst_ref=r1.at[d], send_sem=s1_send.at[k], recv_sem=s1_recv.at[d],
            device_id=(peer, t), device_id_type=MESH)
        c.start()
        sends.append(c)
    for k in range(1, nd):
        src = lax.rem(d + nd - k, nd)
        pltpu.make_async_remote_copy(
            src_ref=s_ref.at[0], dst_ref=r1.at[src], send_sem=s1_send.at[k], recv_sem=s1_recv.at[src],
            device_id=(src, t), device_id_type=MESH).wait_recv()
    own1.wait()
    own2 = pltpu.make_async_copy(r1, r2.at[t], local.at[1])
    own2.start()
    for k in range(1, nt):
        c = pltpu.make_async_remote_copy(
            src_ref=r1, dst_ref=r2.at[t], send_sem=s2_send.at[k], recv_sem=s2_recv.at[t],
            device_id=(d, lax.rem(t + k, nt)), device_id_type=MESH)
        c.start()
        sends.append(c)
    for k in range(1, nt):
        src = lax.rem(t + nt - k, nt)
        pltpu.make_async_remote_copy(
            src_ref=r1, dst_ref=r2.at[src], send_sem=s2_send.at[k], recv_sem=s2_recv.at[src],
            device_id=(d, src), device_id_type=MESH).wait_recv()
    for c in sends:
        c.wait_send()
    own2.wait()
    out_ref[...] = r2[...]


ORDERS = (("x", "y", "z"), ("y", "z", "x"), ("z", "x", "y"))
PARTS = (48, 48, 32)
RING = 4


def _wrap(v):
    return lax.rem(v + RING, RING)


def _gather_kernel(h_ref, g_ref, ssq_ref, tgt_ref, out, t_out, ssem, rsem, psend, precv, lsem,
                   q_buf, t_buf, x_ref, q_send, q_recv, t_send, t_recv):
    d = lax.axis_index("dp")
    t = lax.axis_index("tensor")
    cc = lax.rem(t, 2)
    me = {"x": t // 4, "y": lax.rem(d, 4), "z": (lax.rem(t // 2, 2)) * 2 + d // 4}
    cols = x_ref.shape[1]
    half_cols = cols // 2

    def dev(cd):
        return (lax.rem(cd["z"], 2) * 4 + cd["y"], cd["x"] * 4 + (cd["z"] // 2) * 2 + cc)

    def moved(cd, dim, delta):
        cd = dict(cd)
        cd[dim] = _wrap(cd[dim] + delta)
        return cd

    def slab(r, k, center):
        found = [center]
        for dim in ORDERS[r][:k]:
            found = [dict(cd, **{dim: v}) for cd in found for v in range(RING)]
        return found

    offs = (0, PARTS[0], PARTS[0] + PARTS[1])

    def piece(cd, core, r, half):
        row = (lax.rem(cd["z"], 2) * 4 + cd["y"]) * x_ref.shape[0] + offs[r]
        col = (cd["x"] * 4 + (cd["z"] // 2) * 2 + core) * cols
        if half is None:
            return out.at[pl.ds(pl.multiple_of(row, 16), PARTS[r]), pl.ds(pl.multiple_of(col, cols), cols)]
        col = col + half * half_cols
        return out.at[pl.ds(pl.multiple_of(row, 16), PARTS[r]), pl.ds(pl.multiple_of(col, half_cols), half_cols)]

    partner = (d, t + 1 - 2 * cc)
    barrier = pltpu.get_barrier_semaphore()
    for dim in ("x", "y", "z"):
        for delta in (1, -1):
            pl.semaphore_signal(barrier, inc=1, device_id=dev(moved(me, dim, delta)), device_id_type=MESH)
    pl.semaphore_signal(barrier, inc=1, device_id=partner, device_id_type=MESH)
    nd, nt = 2 * RING, RING * 2 * 2
    for k in range(1, nd):
        pl.semaphore_signal(barrier, inc=1, device_id=(lax.rem(d + k, nd), t), device_id_type=MESH)
    for k in range(1, nt):
        pl.semaphore_signal(barrier, inc=1, device_id=(d, lax.rem(t + k, nt)), device_id_type=MESH)
    pl.semaphore_wait(barrier, 7 + nd - 1 + nt - 1)

    small = []
    for k in range(1, nt):
        c = pltpu.make_async_remote_copy(
            src_ref=ssq_ref, dst_ref=q_buf.at[t], send_sem=q_send.at[k], recv_sem=q_recv.at[t],
            device_id=(d, lax.rem(t + k, nt)), device_id_type=MESH)
        c.start()
        small.append(c)
    for k in range(1, nd):
        c = pltpu.make_async_remote_copy(
            src_ref=tgt_ref, dst_ref=t_buf.at[d], send_sem=t_send.at[k], recv_sem=t_recv.at[d],
            device_id=(lax.rem(d + k, nd), t), device_id_type=MESH)
        c.start()
        small.append(c)
    own_t = pltpu.make_async_copy(tgt_ref, t_buf.at[d], lsem.at[3])
    own_t.start()
    for k in range(1, nt):
        src = lax.rem(t + nt - k, nt)
        pltpu.make_async_remote_copy(
            src_ref=ssq_ref, dst_ref=q_buf.at[src], send_sem=q_send.at[k], recv_sem=q_recv.at[src],
            device_id=(d, src), device_id_type=MESH).wait_recv()
    ssq = ssq_ref[...]
    for k in range(1, nt):
        ssq = ssq + q_buf[lax.rem(t + k, nt)]
    scale = lax.rsqrt(jnp.transpose(ssq)[:, 0:1] / (nt * cols) + 1e-06)
    x_ref[...] = (h_ref[...].astype(jnp.float32) * scale * g_ref[0:1, :]).astype(x_ref.dtype)

    fwd = []

    def to_partner(r, j, cds, half):
        for cd in cds:
            v = piece(cd, cc, r, half)
            pltpu.make_async_remote_copy(
                src_ref=v, dst_ref=v, send_sem=psend.at[r * 13 + j], recv_sem=precv.at[r * 13 + j],
                device_id=partner, device_id_type=MESH).start()
        fwd.append((r * 13 + j, len(cds), r, half))

    own = []
    off = 0
    for r in range(3):
        c = pltpu.make_async_copy(x_ref.at[pl.ds(off, PARTS[r])], piece(me, cc, r, None), lsem.at[r])
        c.start()
        own.append(c)
        off += PARTS[r]
    for r in range(3):
        own[r].wait()
        to_partner(r, 0, [me], None)

    def whole(n, r, half):
        return out.at[pl.ds(0, n * PARTS[r]), pl.ds(0, cols if half is None else half_cols)]

    def recv(group, cds, r, half, src_dev):
        v = whole(len(cds), r, half)
        pltpu.make_async_remote_copy(
            src_ref=v, dst_ref=v, send_sem=ssem.at[group], recv_sem=rsem.at[group],
            device_id=src_dev, device_id_type=MESH).wait_recv()

    sends = []

    def send(group, cds, r, half, dst_dev):
        for cd in cds:
            v = piece(cd, cc, r, half)
            pltpu.make_async_remote_copy(
                src_ref=v, dst_ref=v, send_sem=ssem.at[group], recv_sem=rsem.at[group],
                device_id=dst_dev, device_id_type=MESH).start()
        v = whole(len(cds), r, half)
        sends.append(pltpu.make_async_remote_copy(
            src_ref=v, dst_ref=v, send_sem=ssem.at[group], recv_sem=rsem.at[group],
            device_id=dst_dev, device_id_type=MESH))

    later = []
    for k in range(3):
        for r in range(3):
            dim = ORDERS[r][k]
            for di, delta in enumerate((1, -1)):
                send((r * 3 + k) * 4 + di, slab(r, k, me), r, None, dev(moved(me, dim, delta)))
        for args in later:
            to_partner(*args)
        later = []
        for r in range(3):
            dim = ORDERS[r][k]
            for di, delta in enumerate((1, -1)):
                near = slab(r, k, moved(me, dim, -delta))
                recv((r * 3 + k) * 4 + di, near, r, None, dev(moved(me, dim, -delta)))
            for di, delta in enumerate((1, -1)):
                near = slab(r, k, moved(me, dim, -delta))
                send((r * 3 + k) * 4 + 2 + di, near, r, di, dev(moved(me, dim, delta)))
            for di, delta in enumerate((1, -1)):
                to_partner(r, 1 + 4 * k + di, slab(r, k, moved(me, dim, -delta)), None)
        for r in range(3):
            dim = ORDERS[r][k]
            far = slab(r, k, moved(me, dim, 2))
            for di, delta in enumerate((1, -1)):
                recv((r * 3 + k) * 4 + 2 + di, far, r, di, dev(moved(me, dim, -delta)))
                later.append((r, 3 + 4 * k + di, far, di))
    for args in later:
        to_partner(*args)
    for k in range(1, nd):
        src = lax.rem(d + nd - k, nd)
        pltpu.make_async_remote_copy(
            src_ref=tgt_ref, dst_ref=t_buf.at[src], send_sem=t_send.at[k], recv_sem=t_recv.at[src],
            device_id=(src, t), device_id_type=MESH).wait_recv()
    for c in small:
        c.wait_send()
    own_t.wait()
    t_out[...] = t_buf[...]
    for c in sends:
        c.wait_send()
    for j, n, r, half in fwd:
        v = whole(n, r, half)
        c = pltpu.make_async_remote_copy(
            src_ref=v, dst_ref=v, send_sem=psend.at[j], recv_sem=precv.at[j],
            device_id=partner, device_id_type=MESH)
        c.wait_send()
        c.wait_recv()


def _gather(hidden, gain, ssq_in, tgt_in):
    rows, cols = hidden.shape
    nd, nt = 2 * RING, RING * 2 * 2
    return pl.pallas_call(
        _gather_kernel,
        out_shape=(jax.ShapeDtypeStruct((nd * rows, nt * cols), jnp.bfloat16),
                   jax.ShapeDtypeStruct((nd, 8, rows), jnp.int32)),
        in_specs=[pl.BlockSpec(memory_space=pltpu.VMEM)] * 4,
        out_specs=(pl.BlockSpec(memory_space=pl.ANY), pl.BlockSpec(memory_space=pltpu.VMEM)),
        scratch_shapes=[
            pltpu.SemaphoreType.DMA((36,)), pltpu.SemaphoreType.DMA((36,)),
            pltpu.SemaphoreType.DMA((39,)), pltpu.SemaphoreType.DMA((39,)),
            pltpu.SemaphoreType.DMA((4,)),
            pltpu.VMEM((nt, 8, rows), jnp.float32),
            pltpu.VMEM((nd, 8, rows), jnp.int32),
            pltpu.VMEM((rows, cols), jnp.bfloat16),
            pltpu.SemaphoreType.DMA((nt,)), pltpu.SemaphoreType.DMA((nt,)),
            pltpu.SemaphoreType.DMA((nd,)), pltpu.SemaphoreType.DMA((nd,)),
        ],
        compiler_params=pltpu.CompilerParams(collective_id=2, has_side_effects=True),
    )(hidden, gain, ssq_in, tgt_in)


def _vmem_call(kernel, out_shape, scratch, cid):
    n_out = len(out_shape) if isinstance(out_shape, (tuple, list)) else 1
    out_specs = [pl.BlockSpec(memory_space=pltpu.VMEM)] * n_out
    return pl.pallas_call(
        kernel,
        out_shape=out_shape,
        out_specs=out_specs if n_out > 1 else out_specs[0],
        scratch_shapes=scratch,
        compiler_params=pltpu.CompilerParams(collective_id=cid, has_side_effects=True),
    )


def _body(nd, nt, hidden, norm_gain, head, targets, old_logprob, lengths):
    tok_rows = hidden.shape[0]
    values = hidden.astype(jnp.float32)
    part_sq = jnp.sum(values * values, axis=1)

    ssq_in = jnp.broadcast_to(part_sq[None, :], (8, tok_rows))
    tgt_in = jnp.broadcast_to(targets[None, :], (8, tok_rows))
    gathered, t_all = _gather(hidden, norm_gain[None, :], ssq_in, tgt_in)
    target_all = t_all[:, 0, :].reshape(nd * tok_rows)
    vocab_cols = head.shape[1]
    vocab_start = lax.axis_index(("dp", "tensor")) * vocab_cols
    column = vocab_start + jnp.arange(vocab_cols, dtype=jnp.int32)

    def block_stats(rows, tgt):
        logits = jnp.dot(rows, head, preferred_element_type=jnp.float32)
        top = jnp.max(logits, axis=1)
        total = jnp.sum(jnp.exp(logits - top[:, None]), axis=1)
        hits = column[None, :] == tgt[:, None]
        return top, total, jnp.sum(jnp.where(hits, logits, jnp.float32(0.0)), axis=1)

    split = gathered.shape[0] // 2
    first = block_stats(gathered[:split], target_all[:split])
    second = block_stats(gathered[split:], target_all[split:])
    block_top, block_total, block_pick = (jnp.concatenate([a, b]) for a, b in zip(first, second))

    stacked = jnp.stack([block_top, block_total, block_pick] + [block_top] * 5, axis=0).reshape(8, nd, tok_rows)
    s_in = jnp.transpose(stacked, (1, 0, 2))
    stats = _vmem_call(
        functools.partial(_stats_kernel, nd, nt),
        jax.ShapeDtypeStruct((nt, nd, 8, tok_rows), jnp.float32),
        [pltpu.VMEM((nd, 8, tok_rows), jnp.float32),
         pltpu.VMEM((nt, nd, 8, tok_rows), jnp.float32),
         pltpu.SemaphoreType.DMA((nd,)), pltpu.SemaphoreType.DMA((nd,)),
         pltpu.SemaphoreType.DMA((nt,)), pltpu.SemaphoreType.DMA((nt,)),
         pltpu.SemaphoreType.DMA((2,))],
        1,
    )(s_in)
    pieces = stats.reshape(nt * nd, 8, tok_rows)
    tops = pieces[:, 0, :]
    top = jnp.max(tops, axis=0)
    total = jnp.sum(pieces[:, 1, :] * jnp.exp(tops - top[None, :]), axis=0)
    picked = jnp.sum(pieces[:, 2, :], axis=0)

    seq_count = lengths.shape[0]
    position = jnp.arange(tok_rows // seq_count, dtype=jnp.int32)
    live = (position[None, :] < lengths[:, None]).reshape(-1).astype(jnp.float32)
    logprob = picked - top - jnp.log(total)
    return (live * logprob, live * (logprob - old_logprob))


def solution(mesh):
    nd = mesh.shape["dp"]
    nt = mesh.shape["tensor"]
    in_specs = (
        P("dp", "tensor"),
        P("tensor"),
        P(None, ("dp", "tensor")),
        P("dp"),
        P("dp"),
        P("dp"),
    )
    out_specs = (P("dp"), P("dp"))
    return jax.shard_map(
        functools.partial(_body, nd, nt), mesh=mesh, in_specs=in_specs, out_specs=out_specs, check_vma=False
    )
```

```python
import functools

import jax
import jax.numpy as jnp
from jax import lax
from jax.experimental import pallas as pl
from jax.experimental.pallas import tpu as pltpu
from jax.sharding import PartitionSpec as P

MESH = pl.DeviceIdType.MESH


def _stats_kernel(nd, nt, s_ref, out_ref, r2, send_sem, recv_sem, local):
    n = nd * nt
    d = lax.axis_index("dp")
    t = lax.axis_index("tensor")
    me = d * nt + t
    barrier = pltpu.get_barrier_semaphore()
    for k in range(1, n):
        peer = lax.rem(me + k, n)
        pl.semaphore_signal(barrier, inc=1, device_id=(peer // nt, lax.rem(peer, nt)), device_id_type=MESH)
    pl.semaphore_wait(barrier, n - 1)
    own = pltpu.make_async_copy(s_ref.at[d], r2.at[me], local.at[0])
    own.start()
    for k in range(1, n):
        peer = lax.rem(me + k, n)
        pltpu.make_async_remote_copy(
            src_ref=s_ref.at[peer // nt], dst_ref=r2.at[me], send_sem=send_sem, recv_sem=recv_sem,
            device_id=(peer // nt, lax.rem(peer, nt)), device_id_type=MESH).start()
    whole = pltpu.make_async_remote_copy(
        src_ref=r2.at[pl.ds(0, n - 1)], dst_ref=r2.at[pl.ds(0, n - 1)], send_sem=send_sem, recv_sem=recv_sem,
        device_id=(d, t), device_id_type=MESH)
    whole.wait_recv()
    whole.wait_send()
    own.wait()
    out_ref[...] = r2[...]


ORDERS = (("x", "y", "z"), ("y", "z", "x"), ("z", "x", "y"))
PARTS = (48, 48, 32)
RING = 4


def _wrap(v):
    return lax.rem(v + RING, RING)


def _gather_kernel(h_ref, g_ref, ssq_ref, tgt_ref, out, t_out, ssem, rsem, psend, precv, lsem,
                   q_buf, t_buf, x_ref, q_send, q_recv, t_send, t_recv):
    d = lax.axis_index("dp")
    t = lax.axis_index("tensor")
    cc = lax.rem(t, 2)
    me = {"x": t // 4, "y": lax.rem(d, 4), "z": (lax.rem(t // 2, 2)) * 2 + d // 4}
    cols = x_ref.shape[1]
    half_cols = cols // 2

    def dev(cd):
        return (lax.rem(cd["z"], 2) * 4 + cd["y"], cd["x"] * 4 + (cd["z"] // 2) * 2 + cc)

    def moved(cd, dim, delta):
        cd = dict(cd)
        cd[dim] = _wrap(cd[dim] + delta)
        return cd

    def slab(r, k, center):
        found = [center]
        for dim in ORDERS[r][:k]:
            found = [dict(cd, **{dim: v}) for cd in found for v in range(RING)]
        return found

    offs = (0, PARTS[0], PARTS[0] + PARTS[1])

    def piece(cd, core, r, half):
        row = (lax.rem(cd["z"], 2) * 4 + cd["y"]) * x_ref.shape[0] + offs[r]
        col = (cd["x"] * 4 + (cd["z"] // 2) * 2 + core) * cols
        if half is None:
            return out.at[pl.ds(pl.multiple_of(row, 16), PARTS[r]), pl.ds(pl.multiple_of(col, cols), cols)]
        col = col + half * half_cols
        return out.at[pl.ds(pl.multiple_of(row, 16), PARTS[r]), pl.ds(pl.multiple_of(col, half_cols), half_cols)]

    partner = (d, t + 1 - 2 * cc)
    barrier = pltpu.get_barrier_semaphore()
    for dim in ("x", "y", "z"):
        for delta in (1, -1):
            pl.semaphore_signal(barrier, inc=1, device_id=dev(moved(me, dim, delta)), device_id_type=MESH)
    pl.semaphore_signal(barrier, inc=1, device_id=partner, device_id_type=MESH)
    nd, nt = 2 * RING, RING * 2 * 2
    for k in range(1, nd):
        pl.semaphore_signal(barrier, inc=1, device_id=(lax.rem(d + k, nd), t), device_id_type=MESH)
    for k in range(1, nt):
        pl.semaphore_signal(barrier, inc=1, device_id=(d, lax.rem(t + k, nt)), device_id_type=MESH)
    pl.semaphore_wait(barrier, 7 + nd - 1 + nt - 1)

    small = []
    for k in range(1, nt):
        c = pltpu.make_async_remote_copy(
            src_ref=ssq_ref, dst_ref=q_buf.at[t], send_sem=q_send.at[k], recv_sem=q_recv.at[t],
            device_id=(d, lax.rem(t + k, nt)), device_id_type=MESH)
        c.start()
        small.append(c)
    for k in range(1, nd):
        c = pltpu.make_async_remote_copy(
            src_ref=tgt_ref, dst_ref=t_buf.at[d], send_sem=t_send.at[k], recv_sem=t_recv.at[d],
            device_id=(lax.rem(d + k, nd), t), device_id_type=MESH)
        c.start()
        small.append(c)
    own_t = pltpu.make_async_copy(tgt_ref, t_buf.at[d], lsem.at[3])
    own_t.start()
    for k in range(1, nt):
        src = lax.rem(t + nt - k, nt)
        pltpu.make_async_remote_copy(
            src_ref=ssq_ref, dst_ref=q_buf.at[src], send_sem=q_send.at[k], recv_sem=q_recv.at[src],
            device_id=(d, src), device_id_type=MESH).wait_recv()
    ssq = ssq_ref[...]
    for k in range(1, nt):
        ssq = ssq + q_buf[lax.rem(t + k, nt)]
    scale = lax.rsqrt(jnp.transpose(ssq)[:, 0:1] / (nt * cols) + 1e-06)
    x_ref[...] = (h_ref[...].astype(jnp.float32) * scale * g_ref[0:1, :]).astype(x_ref.dtype)

    fwd = []

    def to_partner(r, j, cds, half):
        for cd in cds:
            v = piece(cd, cc, r, half)
            pltpu.make_async_remote_copy(
                src_ref=v, dst_ref=v, send_sem=psend.at[r * 13 + j], recv_sem=precv.at[r * 13 + j],
                device_id=partner, device_id_type=MESH).start()
        fwd.append((r * 13 + j, len(cds), r, half))

    own = []
    off = 0
    for r in range(3):
        c = pltpu.make_async_copy(x_ref.at[pl.ds(off, PARTS[r])], piece(me, cc, r, None), lsem.at[r])
        c.start()
        own.append(c)
        off += PARTS[r]
    for r in range(3):
        own[r].wait()
        to_partner(r, 0, [me], None)

    def whole(n, r, half):
        return out.at[pl.ds(0, n * PARTS[r]), pl.ds(0, cols if half is None else half_cols)]

    def recv(group, cds, r, half, src_dev):
        v = whole(len(cds), r, half)
        pltpu.make_async_remote_copy(
            src_ref=v, dst_ref=v, send_sem=ssem.at[group], recv_sem=rsem.at[group],
            device_id=src_dev, device_id_type=MESH).wait_recv()

    sends = []

    def send(group, cds, r, half, dst_dev):
        for cd in cds:
            v = piece(cd, cc, r, half)
            pltpu.make_async_remote_copy(
                src_ref=v, dst_ref=v, send_sem=ssem.at[group], recv_sem=rsem.at[group],
                device_id=dst_dev, device_id_type=MESH).start()
        v = whole(len(cds), r, half)
        sends.append(pltpu.make_async_remote_copy(
            src_ref=v, dst_ref=v, send_sem=ssem.at[group], recv_sem=rsem.at[group],
            device_id=dst_dev, device_id_type=MESH))

    later = []
    for k in range(3):
        for r in range(3):
            dim = ORDERS[r][k]
            for di, delta in enumerate((1, -1)):
                send((r * 3 + k) * 4 + di, slab(r, k, me), r, None, dev(moved(me, dim, delta)))
        for args in later:
            to_partner(*args)
        later = []
        for r in range(3):
            dim = ORDERS[r][k]
            for di, delta in enumerate((1, -1)):
                near = slab(r, k, moved(me, dim, -delta))
                recv((r * 3 + k) * 4 + di, near, r, None, dev(moved(me, dim, -delta)))
            for di, delta in enumerate((1, -1)):
                near = slab(r, k, moved(me, dim, -delta))
                send((r * 3 + k) * 4 + 2 + di, near, r, di, dev(moved(me, dim, delta)))
            for di, delta in enumerate((1, -1)):
                to_partner(r, 1 + 4 * k + di, slab(r, k, moved(me, dim, -delta)), None)
        for r in range(3):
            dim = ORDERS[r][k]
            far = slab(r, k, moved(me, dim, 2))
            for di, delta in enumerate((1, -1)):
                recv((r * 3 + k) * 4 + 2 + di, far, r, di, dev(moved(me, dim, -delta)))
                later.append((r, 3 + 4 * k + di, far, di))
    for args in later:
        to_partner(*args)
    for k in range(1, nd):
        src = lax.rem(d + nd - k, nd)
        pltpu.make_async_remote_copy(
            src_ref=tgt_ref, dst_ref=t_buf.at[src], send_sem=t_send.at[k], recv_sem=t_recv.at[src],
            device_id=(src, t), device_id_type=MESH).wait_recv()
    for c in small:
        c.wait_send()
    own_t.wait()
    t_out[...] = t_buf[...]
    for c in sends:
        c.wait_send()
    for j, n, r, half in fwd:
        v = whole(n, r, half)
        c = pltpu.make_async_remote_copy(
            src_ref=v, dst_ref=v, send_sem=psend.at[j], recv_sem=precv.at[j],
            device_id=partner, device_id_type=MESH)
        c.wait_send()
        c.wait_recv()


def _gather(hidden, gain, ssq_in, tgt_in):
    rows, cols = hidden.shape
    nd, nt = 2 * RING, RING * 2 * 2
    return pl.pallas_call(
        _gather_kernel,
        out_shape=(jax.ShapeDtypeStruct((nd * rows, nt * cols), jnp.bfloat16),
                   jax.ShapeDtypeStruct((nd, 8, rows), jnp.int32)),
        in_specs=[pl.BlockSpec(memory_space=pltpu.VMEM)] * 4,
        out_specs=(pl.BlockSpec(memory_space=pl.ANY), pl.BlockSpec(memory_space=pltpu.VMEM)),
        scratch_shapes=[
            pltpu.SemaphoreType.DMA((36,)), pltpu.SemaphoreType.DMA((36,)),
            pltpu.SemaphoreType.DMA((39,)), pltpu.SemaphoreType.DMA((39,)),
            pltpu.SemaphoreType.DMA((4,)),
            pltpu.VMEM((nt, 8, rows), jnp.float32),
            pltpu.VMEM((nd, 8, rows), jnp.int32),
            pltpu.VMEM((rows, cols), jnp.bfloat16),
            pltpu.SemaphoreType.DMA((nt,)), pltpu.SemaphoreType.DMA((nt,)),
            pltpu.SemaphoreType.DMA((nd,)), pltpu.SemaphoreType.DMA((nd,)),
        ],
        compiler_params=pltpu.CompilerParams(collective_id=2, has_side_effects=True),
    )(hidden, gain, ssq_in, tgt_in)


def _vmem_call(kernel, out_shape, scratch, cid):
    n_out = len(out_shape) if isinstance(out_shape, (tuple, list)) else 1
    out_specs = [pl.BlockSpec(memory_space=pltpu.VMEM)] * n_out
    return pl.pallas_call(
        kernel,
        out_shape=out_shape,
        out_specs=out_specs if n_out > 1 else out_specs[0],
        scratch_shapes=scratch,
        compiler_params=pltpu.CompilerParams(collective_id=cid, has_side_effects=True),
    )


def _body(nd, nt, hidden, norm_gain, head, targets, old_logprob, lengths):
    tok_rows = hidden.shape[0]
    values = hidden.astype(jnp.float32)
    part_sq = jnp.sum(values * values, axis=1)

    ssq_in = jnp.broadcast_to(part_sq[None, :], (8, tok_rows))
    tgt_in = jnp.broadcast_to(targets[None, :], (8, tok_rows))
    gathered, t_all = _gather(hidden, norm_gain[None, :], ssq_in, tgt_in)
    target_all = t_all[:, 0, :].reshape(nd * tok_rows)
    logits = jnp.dot(gathered, head, preferred_element_type=jnp.float32)
    vocab_cols = head.shape[1]
    vocab_start = lax.axis_index(("dp", "tensor")) * vocab_cols
    block_top = jnp.max(logits, axis=1)
    block_total = jnp.sum(jnp.exp(logits - block_top[:, None]), axis=1)
    column = vocab_start + jnp.arange(vocab_cols, dtype=jnp.int32)
    hits = column[None, :] == target_all[:, None]
    block_pick = jnp.sum(jnp.where(hits, logits, jnp.float32(0.0)), axis=1)

    stacked = jnp.stack([block_top, block_total, block_pick] + [block_top] * 5, axis=0).reshape(8, nd, tok_rows)
    s_in = jnp.transpose(stacked, (1, 0, 2))
    stats = _vmem_call(
        functools.partial(_stats_kernel, nd, nt),
        jax.ShapeDtypeStruct((nt * nd, 8, tok_rows), jnp.float32),
        [pltpu.VMEM((nt * nd, 8, tok_rows), jnp.float32),
         pltpu.SemaphoreType.DMA, pltpu.SemaphoreType.DMA,
         pltpu.SemaphoreType.DMA((1,))],
        1,
    )(s_in)
    pieces = stats.reshape(nt * nd, 8, tok_rows)
    tops = pieces[:, 0, :]
    top = jnp.max(tops, axis=0)
    total = jnp.sum(pieces[:, 1, :] * jnp.exp(tops - top[None, :]), axis=0)
    picked = jnp.sum(pieces[:, 2, :], axis=0)

    seq_count = lengths.shape[0]
    position = jnp.arange(tok_rows // seq_count, dtype=jnp.int32)
    live = (position[None, :] < lengths[:, None]).reshape(-1).astype(jnp.float32)
    logprob = picked - top - jnp.log(total)
    return (live * logprob, live * (logprob - old_logprob))


def solution(mesh):
    nd = mesh.shape["dp"]
    nt = mesh.shape["tensor"]
    in_specs = (
        P("dp", "tensor"),
        P("tensor"),
        P(None, ("dp", "tensor")),
        P("dp"),
        P("dp"),
        P("dp"),
    )
    out_specs = (P("dp"), P("dp"))
    return jax.shard_map(
        functools.partial(_body, nd, nt), mesh=mesh, in_specs=in_specs, out_specs=out_specs, check_vma=False
    )
```
